256 devices in a mesh: seq: 32 (over y, x, core), chan: 8 (over z).
Axes of the slice: x: 4, y: 4, z: 8, core: 2. Of those that a mesh axis runs over, the one named last changes fastest.
Arguments:
- conv_in: bfloat16 [32, 512, 512], P(None, 'seq', 'chan'), may hold values from -4 to 4
- conv_gate: bfloat16 [32, 512, 512], P(None, 'seq', 'chan'), may hold values from -4 to 4
- long_filter: float32 [32, 512, 512], P(None, 'seq', 'chan'), may hold values from -1.1 to 1.1
- skip_gain: float32 [512], P('chan'), may hold values from 0.5 to 1.5
- queries: bfloat16 [32, 512, 1024], P(None, 'seq', 'chan'), may hold values from -40 to 40
- keys_in: bfloat16 [32, 512, 1024], P(None, 'seq', 'chan'), may hold values from -40 to 40
- w_value: bfloat16 [512, 1024], P(None, 'chan'), may hold values from -0.25 to 0.25
Outputs:
- conv_out: bfloat16 [32, 512, 512], P(None, 'seq', 'chan')
- attended: bfloat16 [32, 512, 1024], P(None, 'seq', 'chan')
The draws below stay inside these ranges and needn't reach their ends.
All inputs are finite; a program needn't handle non-finite values.
Results may differ from the reference program's by a relative error of at most 0.015.
Values may be sent and summed in bfloat16 or wider, within the bound.
A program may use at most 64 MiB of HBM per device.

```python
import math
import jax
import jax.numpy as jnp
from jax import lax

T_DEV = 512
CH = 512
HD = 128
SEQ_LEN = 16384
HEADS = 8
N_SEQ = 32


def paired_rows(key):
    base = jax.random.fold_in(key, 7)
    key_query, key_keys = jax.random.split(base, 2)
    width_all = HEADS * HD
    shape_all = (SEQ_LEN // T_DEV, T_DEV, width_all)
    query_draw = jnp.clip(jax.random.normal(key_query, shape_all, jnp.float32), -4.0, 4.0) * 1.6
    key_draw = jnp.clip(jax.random.normal(key_keys, shape_all, jnp.float32), -4.0, 4.0) * 1.6
    return (query_draw, key_draw)


def draw_queries(key, part):
    return paired_rows(key)[0].astype(jnp.bfloat16)


def draw_keys_in(key, part):
    return paired_rows(key)[1].astype(jnp.bfloat16)


def draw_long_filter(key, part):
    base = jax.random.fold_in(key, 11)
    key_rate, key_noise = jax.random.split(base)
    shape_all = (SEQ_LEN // T_DEV, T_DEV, CH)
    position = jnp.arange(SEQ_LEN // T_DEV, dtype=jnp.float32)[:, None, None] * T_DEV + jnp.arange(T_DEV, dtype=jnp.float32)[None, :, None]
    log_rate = jax.random.uniform(key_rate, (CH,), jnp.float32, math.log(0.3 / SEQ_LEN), math.log(1.0 / 30.0))
    noise = jnp.clip(jax.random.normal(key_noise, shape_all, jnp.float32), -4.0, 4.0)
    decay_rate = jnp.exp(log_rate)
    amplitude = jnp.sqrt(2.0 * decay_rate + 1.0 / SEQ_LEN)
    return amplitude * noise * jnp.exp(-decay_rate * position)


def levels(key, dims, cuts, low, high):
    factor_of = 1.0
    for axis_at, shards_of in cuts:
        draws = jax.random.uniform(jax.random.fold_in(jax.random.fold_in(key, 6), axis_at), (shards_of,), jnp.float32, low / len(cuts), high / len(cuts))
        factor_of = factor_of * jnp.repeat(jnp.exp(draws), dims[axis_at] // shards_of).reshape((-1,) + (1,) * (len(dims) - 1 - axis_at))
    return factor_of


def bell_draw(stream_key, extent, scale, most, cuts=(), held_as=jnp.bfloat16):
    drawn = jax.random.normal(stream_key, extent, jnp.float32) * scale
    if len(cuts) > 0:
        drawn = levels(stream_key, extent, cuts, -0.22, 0.18) * drawn
    return jnp.clip(drawn, min=-most, max=most).astype(held_as)


def setup_inputs(seed: int = 0) -> dict:
    key_of = jax.random.split(jax.random.key(seed), 8)
    conv_in = bell_draw(key_of[0], (N_SEQ, T_DEV, CH), 1.0, 4.0, ((1, 32), (2, 8)))
    conv_gate = bell_draw(key_of[1], (N_SEQ, T_DEV, CH), 1.0, 4.0, ((1, 32), (2, 8)))
    long_filter = draw_long_filter(jax.random.fold_in(key_of[7], 71), 0)
    skip_gain = jnp.clip(0.5 + 1.0 * jax.random.uniform(key_of[3], (CH,), jnp.float32) ** levels(key_of[3], (CH,), ((0, 8),), -0.2, 0.2), 0.5, 1.5)
    queries = draw_queries(jax.random.fold_in(key_of[7], 71), 0)
    keys_in = draw_keys_in(jax.random.fold_in(key_of[7], 71), 0)
    w_value = bell_draw(key_of[6], (CH, HEADS * HD), CH ** -0.5, 0.25, ((1, 8),))
    return dict(conv_in=conv_in, conv_gate=conv_gate, long_filter=long_filter, skip_gain=skip_gain, queries=queries, keys_in=keys_in, w_value=w_value)


def attend_block(query_block, first_row, key_head, value_head):
    block_rows = query_block.shape[0]
    length_all = key_head.shape[0]
    scores = jnp.dot(query_block, key_head.T, preferred_element_type=jnp.float32) * (1.0 / math.sqrt(key_head.shape[1]))
    query_pos = first_row + jnp.arange(block_rows, dtype=jnp.int32)
    key_pos = jnp.arange(length_all, dtype=jnp.int32)
    allowed = key_pos[None, :] <= query_pos[:, None]
    scores = jnp.where(allowed, scores, -1e+30)
    row_best = lax.optimization_barrier(jnp.max(scores, axis=1, keepdims=True))
    weights = jnp.where(allowed, jnp.exp(scores - row_best), 0.0)
    row_total = lax.optimization_barrier(jnp.sum(weights, axis=1, keepdims=True))
    summed = jnp.dot(weights.astype(jnp.bfloat16), value_head, preferred_element_type=jnp.float32)
    return (summed / row_total).astype(jnp.bfloat16)

def reference(conv_in, conv_gate, long_filter, skip_gain, queries, keys_in, w_value):
    blocks, slab_rows, channels = conv_in.shape
    seq_total = blocks * slab_rows
    signal = conv_in.reshape(seq_total, channels).astype(jnp.float32)
    filter_taps = long_filter.reshape(seq_total, channels)
    spectrum = jnp.fft.rfft(signal, 2 * seq_total, axis=0) * jnp.fft.rfft(filter_taps, 2 * seq_total, axis=0)
    convolved = jnp.fft.irfft(spectrum, 2 * seq_total, axis=0)[:seq_total]
    mixed = (convolved + skip_gain[None, :] * signal) * conv_gate.reshape(seq_total, channels).astype(jnp.float32)
    conv_out = mixed.astype(jnp.bfloat16)
    values = jnp.dot(conv_out, w_value, preferred_element_type=jnp.float32).astype(jnp.bfloat16)
    width_all = queries.shape[2]
    head_count = width_all // HD
    block_rows = math.gcd(seq_total, 512)

    def split_heads(matrix):
        return matrix.reshape(seq_total, head_count, HD).transpose(1, 0, 2)

    def per_head(packed):
        query_head, key_head, value_head = packed
        query_blocks = query_head.reshape(seq_total // block_rows, block_rows, HD)
        starts = jnp.arange(seq_total // block_rows, dtype=jnp.int32) * block_rows

        def one_block(blocked):
            return attend_block(blocked[0], blocked[1], key_head, value_head)
        result = lax.map(one_block, (query_blocks, starts))
        return result.reshape(seq_total, HD)
    attended = lax.map(per_head, (split_heads(queries.reshape(seq_total, width_all)), split_heads(keys_in.reshape(seq_total, width_all)), split_heads(values)))
    attended = attended.transpose(1, 0, 2).reshape(blocks, slab_rows, width_all)
    return (conv_out.reshape(blocks, slab_rows, channels), attended)
```

```python
import math

import jax
import jax.numpy as jnp
from jax import lax
from jax.experimental import pallas as pl
from jax.experimental.pallas import tpu as pltpu
from jax.sharding import PartitionSpec as P

MESH = pl.DeviceIdType.MESH
F32 = jnp.float32
BF16 = jnp.bfloat16
VM = pltpu.VMEM


def device_at(seq, chan):
    return (jnp.int32(seq), jnp.int32(chan))


def signal(target):
    pl.semaphore_signal(
        pltpu.get_barrier_semaphore(), inc=1, device_id=target, device_id_type=MESH
    )


def remote(src, dst, send, recv, target):
    return pltpu.make_async_remote_copy(
        src_ref=src,
        dst_ref=dst,
        send_sem=send,
        recv_sem=recv,
        device_id=target,
        device_id_type=MESH,
    )


def exchange_kernel(n, along_seq, spread, src, dst, send, recv, own):
    seq = lax.axis_index("seq")
    chan = lax.axis_index("chan")
    me = seq if along_seq else chan

    def peer(step):
        other = lax.rem(me + step, n)
        return other, (device_at(other, chan) if along_seq else device_at(seq, other))

    def greet(step, carry):
        signal(peer(step)[1])
        return carry

    lax.fori_loop(1, n, greet, 0)
    local = pltpu.make_async_copy(src if spread else src.at[me], dst.at[me], own)
    local.start()
    pl.semaphore_wait(pltpu.get_barrier_semaphore(), n - 1)

    def post(step, carry):
        other, target = peer(step)
        remote(
            src if spread else src.at[other], dst.at[me], send.at[step], recv.at[step], target
        ).start()
        return carry

    lax.fori_loop(1, n, post, 0)

    def finish(step, carry):
        other, target = peer(step)
        back = lax.rem(me + n - step, n)
        done = remote(
            src if spread else src.at[other], dst.at[back], send.at[step], recv.at[step], target
        )
        done.wait()
        return carry

    lax.fori_loop(1, n, finish, 0)
    local.wait()


def all_to_all(blocks, collective):
    n = blocks.shape[0]

    def kernel(src, dst, send, recv, own):
        exchange_kernel(n, True, False, src, dst, send, recv, own)

    return pl.pallas_call(
        kernel,
        out_shape=jax.ShapeDtypeStruct(blocks.shape, blocks.dtype),
        in_specs=[pl.BlockSpec(memory_space=VM)],
        out_specs=pl.BlockSpec(memory_space=VM),
        scratch_shapes=[
            pltpu.SemaphoreType.DMA((n,)),
            pltpu.SemaphoreType.DMA((n,)),
            pltpu.SemaphoreType.DMA,
        ],
        compiler_params=pltpu.CompilerParams(collective_id=collective, has_side_effects=True),
    )(blocks)


def project_values(mixed, w_value, n_chan):
    rows, tokens = mixed.shape

    def kernel(src, w_ref, out, held, send, recv, own):
        exchange_kernel(n_chan, False, True, src, held, send, recv, own)
        out[...] = lax.dot_general(
            held[...].reshape(n_chan * rows, tokens),
            w_ref[...],
            (((0,), (0,)), ((), ())),
            preferred_element_type=F32,
        ).astype(out.dtype)

    return pl.pallas_call(
        kernel,
        out_shape=jax.ShapeDtypeStruct((tokens, w_value.shape[1]), BF16),
        in_specs=[pl.BlockSpec(memory_space=VM)] * 2,
        out_specs=pl.BlockSpec(memory_space=VM),
        scratch_shapes=[
            pltpu.VMEM((n_chan, rows, tokens), BF16),
            pltpu.SemaphoreType.DMA((n_chan,)),
            pltpu.SemaphoreType.DMA((n_chan,)),
            pltpu.SemaphoreType.DMA,
        ],
        compiler_params=pltpu.CompilerParams(collective_id=2, has_side_effects=True),
    )(mixed, w_value)


SIDE = 4
COPIES = 26


class Gather:
    def __init__(self, own_ref, buf, send, recv, own_sem):
        seq = lax.axis_index("seq")
        self.chan = lax.axis_index("chan")
        self.own_ref, self.buf, self.send, self.recv, self.own_sem = (
            own_ref, buf, send, recv, own_sem
        )
        self.core = lax.rem(seq, 2)
        self.x = lax.rem(seq // 2, SIDE)
        self.y = seq // (2 * SIDE)
        self.half = own_ref.shape[0] // 2

    def at(self, y, x, core):
        return device_at((y * SIDE + x) * 2 + core, self.chan)

    def step(self, half, phase, by):
        along_x = (half == 0) == (phase == 1)
        if along_x:
            return self.at(self.y, lax.rem(self.x + by + SIDE, SIDE), self.core)
        return self.at(lax.rem(self.y + by + SIDE, SIDE), self.x, self.core)

    def block(self, half, phase, by):
        rows = pl.ds(half * self.half, self.half)
        along_x = (half == 0) == (phase == 1)
        y, x = self.y, self.x
        if along_x:
            x = lax.rem(x + by + SIDE, SIDE)
        else:
            y = lax.rem(y + by + SIDE, SIDE)
        return y, x, along_x, rows

    def one(self, half, by):
        y, x, _, rows = self.block(half, 1, by)
        return self.buf.at[y, x, self.core, rows]

    def row(self, half, by, core=None, part=None):
        y, x, along_x, rows = self.block(half, 2, by)
        core = self.core if core is None else core
        if part is not None:
            quarter = self.half // 2
            rows = pl.ds(half * self.half + part * quarter, quarter)
        if along_x:
            return self.buf.at[:, x, core, rows]
        return self.buf.at[y, :, core, rows]

    def sems(self, half, number):
        index = half * 13 + number
        return self.send.at[index], self.recv.at[index]

    def greet(self):
        for by in (1, 2, 3):
            signal(self.step(0, 1, by))
            signal(self.step(1, 1, by))
        signal(self.at(self.y, self.x, 1 - self.core))
        self.local = pltpu.make_async_copy(
            self.own_ref, self.buf.at[self.y, self.x, self.core], self.own_sem
        )
        self.local.start()
        pl.semaphore_wait(pltpu.get_barrier_semaphore(), 7)


    def first(self, half, i, landing=False):
        by = (1, -1, 2)[i]
        rows = pl.ds(half * self.half, self.half)
        dst = self.one(half, -by) if landing else self.one(half, 0)
        return remote(self.own_ref.at[rows], dst, *self.sems(half, i), self.step(half, 1, by))

    def second(self, half, i, landing=False):
        by = (1, -1)[i]
        dst = self.row(half, -by) if landing else self.row(half, 0)
        return remote(self.row(half, 0), dst, *self.sems(half, 3 + i), self.step(half, 2, by))

    def relay(self, half, i, landing=False):
        by = (1, -1)[i]
        src = self.row(half, -by, part=i)
        dst = self.row(half, 2, part=i) if landing else src
        return remote(src, dst, *self.sems(half, 5 + i), self.step(half, 2, by))

    def across(self, half, i, landing=False):
        by, part = ((0, None), (-1, None), (1, None), (2, 0), (2, 1))[i]
        src = self.row(half, by, part=part)
        dst = self.row(half, by, core=1 - self.core, part=part) if landing else src
        return remote(
            src, dst, *self.sems(half, 7 + i), self.at(self.y, self.x, 1 - self.core)
        )

    def start(self):
        self.greet()
        for i in range(3):
            for half in range(2):
                self.first(half, i).start()

    def middle(self):
        self.local.wait()
        for half in range(2):
            for i in range(3):
                self.first(half, i, True).wait_recv()
            for i in range(2):
                self.second(half, i).start()
        for half in range(2):
            self.across(half, 0).start()

    def late(self):
        for i in range(2):
            for half in range(2):
                self.second(half, i, True).wait_recv()
                self.relay(half, i).start()
        for i in range(2):
            for half in range(2):
                self.across(half, 1 + i).start()

    def last(self):
        for i in range(2):
            for half in range(2):
                self.relay(half, i, True).wait_recv()
                self.across(half, 3 + i).start()

    def end(self):
        for half in range(2):
            for i in range(5):
                self.across(half, i, True).wait_recv()
        for half in range(2):
            for i in range(3):
                self.first(half, i).wait_send()
            for i in range(2):
                self.second(half, i).wait_send()
                self.relay(half, i).wait_send()
            for i in range(5):
                self.across(half, i).wait_send()


def gather_scratch():
    return [
        pltpu.SemaphoreType.DMA((COPIES,)),
        pltpu.SemaphoreType.DMA((COPIES,)),
        pltpu.SemaphoreType.DMA,
    ]


TILE = 128
GROUP = 16


def spread_taps(h_ref, base, ch):
    wide = jnp.broadcast_to(h_ref[ch], (8, h_ref.shape[2])).astype(F32)
    sub = lax.broadcasted_iota(jnp.int32, wide.shape, 0)
    for bit in (1, 2, 4):
        wide = jnp.where((sub & bit) != 0, pltpu.roll(wide, bit, 1), wide)
    base[...] = wide


def spread_signal(x_ref, shifted, ch):
    x = x_ref[ch].astype(F32)
    row = lax.broadcasted_iota(jnp.int32, x.shape, 0)
    for k in range(GROUP):
        moved = x if k == 0 else jnp.where(row >= k, pltpu.roll(x, k, 0), 0.0)
        lanes = pl.ds((k % 2) * TILE, TILE)
        shifted[k // 2, :, lanes] = moved.astype(BF16)


def toeplitz(base, lane):
    parts = []
    for half in range(2):
        window = base[:, pl.ds(pl.multiple_of(lane + half * TILE, TILE), 2 * TILE)]
        for u in range(TILE // 8):
            moved = window if u == 0 else pltpu.roll(window, 8 * u, 1)
            parts.append(moved[:, TILE:])
    return jnp.concatenate(parts, axis=0).astype(BF16)


def convolve_channel(x_ref, h_ref, y_ref, base, shifted, total, ch):
    blocks = x_ref.shape[1]
    spread_taps(h_ref, base, ch)
    spread_signal(x_ref, shifted, ch)
    for g in range(blocks // GROUP):
        rows = blocks - GROUP * g

        def pair(kk, acc, g=g, rows=rows):
            block = toeplitz(base, (GROUP * g + 2 * kk) * TILE)
            left = shifted[kk, pl.ds(0, rows), :]
            return acc + jnp.dot(left, block, preferred_element_type=F32)

        acc = lax.fori_loop(0, GROUP // 2, pair, jnp.zeros((rows, TILE), F32), unroll=2)
        if g == 0:
            total[...] = acc
        else:
            total[pl.ds(GROUP * g, rows), :] += acc
    y_ref[ch] = total[...].astype(BF16)


def conv_and_keys(x, h, keys):
    tokens, head = keys.shape

    def kernel(x_ref, h_ref, k_ref, y_ref, buf, base, shifted, total, send, recv, own):
        gather = Gather(k_ref, buf, send, recv, own)
        gather.start()
        spare = x_ref.shape[0]
        convolve_channel(x_ref, h_ref, y_ref, base, shifted, total, 0)
        gather.middle()
        for ch in range(1, spare):
            convolve_channel(x_ref, h_ref, y_ref, base, shifted, total, ch)
        gather.late()
        gather.last()
        gather.end()

    blocks = x.shape[1]
    return pl.pallas_call(
        kernel,
        out_shape=(
            jax.ShapeDtypeStruct(x.shape, BF16),
            jax.ShapeDtypeStruct((SIDE, SIDE, 2, tokens, head), BF16),
        ),
        in_specs=[pl.BlockSpec(memory_space=VM)] * 3,
        out_specs=(pl.BlockSpec(memory_space=VM),) * 2,
        scratch_shapes=[
            pltpu.VMEM((8, h.shape[2]), F32),
            pltpu.VMEM((GROUP // 2, blocks, 2 * TILE), BF16),
            pltpu.VMEM((blocks, TILE), F32),
        ]
        + gather_scratch(),
        compiler_params=pltpu.CompilerParams(collective_id=1, has_side_effects=True),
    )(x, h, keys)


QROWS = 128


def key_block(buf, index, slab):
    part = buf[:, :, :, pl.ds(pl.multiple_of(index * slab, slab), slab), :]
    return part.reshape(2 * SIDE * SIDE * slab, part.shape[-1])


def fold(values, combine):
    out = values[:, :TILE]
    for start in range(TILE, values.shape[1], TILE):
        out = combine(out, values[:, start : start + TILE])
    return out


def attend(queries, keys, values, slab):
    tokens, head = queries.shape
    scale = math.log2(math.e) / math.sqrt(head)
    width = 2 * SIDE * SIDE * slab
    per_tile = QROWS // slab
    tiles = tokens // QROWS

    def kernel(q_ref, k_buf, v_ref, out, buf, weights, totals, send, recv, own):
        first_row = lax.axis_index("seq") * slab
        row = lax.broadcasted_iota(jnp.int32, (QROWS, width), 0)
        lane = lax.broadcasted_iota(jnp.int32, (QROWS, width), 1)

        def scores(q, block):
            return lax.dot_general(
                q, key_block(k_buf, block, slab), (((1,), (1,)), ((), ())),
                preferred_element_type=F32,
            )

        def allowed(tile, block):
            return (block - tile * per_tile) * width + lane <= (
                (row // slab) * width + first_row + row % slab
            )

        def weigh(tile):
            q = q_ref[pl.ds(tile * QROWS, QROWS), :]
            whole = tile * per_tile

            def best_whole(block, best):
                return jnp.maximum(best, fold(scores(q, block), jnp.maximum))

            def best_edge(block, best):
                s = jnp.where(allowed(tile, block), scores(q, block), -1e30)
                return jnp.maximum(best, fold(s, jnp.maximum))

            best = jnp.full((QROWS, TILE), -1e30, F32)
            best = lax.fori_loop(0, whole, best_whole, best)
            best = lax.fori_loop(whole, whole + per_tile, best_edge, best)
            best = jnp.max(best, axis=1, keepdims=True)

            def put(block, w):
                lanes = pl.ds(pl.multiple_of(block * width, width), width)
                weights[pl.ds(tile * QROWS, QROWS), lanes] = w.astype(BF16)

            def weigh_whole(block, total):
                w = jnp.exp2((scores(q, block) - best) * scale)
                put(block, w)
                return total + fold(w, jnp.add)

            def weigh_edge(block, total):
                w = jnp.exp2((scores(q, block) - best) * scale)
                w = jnp.where(allowed(tile, block), w, 0.0)
                put(block, w)
                return total + fold(w, jnp.add)

            total = jnp.zeros((QROWS, TILE), F32)
            total = lax.fori_loop(0, whole, weigh_whole, total)
            total = lax.fori_loop(whole, whole + per_tile, weigh_edge, total)
            totals[pl.ds(tile * QROWS, QROWS), :] = jnp.broadcast_to(
                jnp.sum(total, axis=1, keepdims=True), (QROWS, TILE)
            )

        gather = Gather(v_ref, buf, send, recv, own)
        gather.start()
        weigh(0)
        gather.middle()
        weigh(1)
        weigh(2)
        gather.late()
        weigh(3)
        gather.last()
        gather.end()

        for tile in range(tiles):
            rows = pl.ds(tile * QROWS, QROWS)

            def add(block, acc, rows=rows):
                lanes = pl.ds(pl.multiple_of(block * width, width), width)
                return acc + jnp.dot(
                    weights[rows, lanes], key_block(buf, block, slab), preferred_element_type=F32
                )

            acc = lax.fori_loop(
                0, (tile + 1) * per_tile, add, jnp.zeros((QROWS, head), F32), unroll=4
            )
            out[rows, :] = (acc / totals[rows, :]).astype(BF16)

    return pl.pallas_call(
        kernel,
        out_shape=jax.ShapeDtypeStruct((tokens, head), BF16),
        in_specs=[pl.BlockSpec(memory_space=VM)] * 3,
        out_specs=pl.BlockSpec(memory_space=VM),
        scratch_shapes=[
            pltpu.VMEM((SIDE, SIDE, 2, tokens, head), BF16),
            pltpu.VMEM((tokens, tokens * 2 * SIDE * SIDE), BF16),
            pltpu.VMEM((tokens, TILE), F32),
        ]
        + gather_scratch(),
        compiler_params=pltpu.CompilerParams(collective_id=3, has_side_effects=True),
    )(queries, keys, values)


def body(n_chan, conv_in, conv_gate, long_filter, skip_gain, queries, keys_in, w_value):
    blocks, slab, channels = conv_in.shape
    tokens = blocks * slab
    n_seq = 2 * SIDE * SIDE
    each = channels // n_seq
    length = tokens * n_seq
    lines = tokens // TILE
    signal_t = conv_in.reshape(tokens, channels).T
    taps_t = long_filter.reshape(tokens, channels).astype(BF16).T
    packed = jnp.stack(
        [signal_t.reshape(n_seq, each, tokens), taps_t.reshape(n_seq, each, tokens)], axis=1
    ).reshape(n_seq, 2 * each * lines, TILE)
    got = all_to_all(packed, 0)
    whole = (
        got.reshape(n_seq, 2, each, blocks, slab).transpose(1, 2, 3, 0, 4).reshape(2, each, length)
    )
    x = whole[0].reshape(each, length // TILE, TILE)
    h = jnp.pad(whole[1].astype(F32), ((0, 0), (TILE, 0))).reshape(each, 1, length + TILE)
    y, keys = conv_and_keys(x, h, keys_in.reshape(tokens, -1))
    back = (
        y.reshape(each, blocks, n_seq, slab)
        .transpose(2, 0, 1, 3)
        .reshape(n_seq, each * lines, TILE)
    )
    convolved = all_to_all(back, 4).reshape(channels, tokens).astype(F32)
    gate_t = conv_gate.reshape(tokens, channels).T
    mixed_t = (
        (convolved + skip_gain[:, None] * signal_t.astype(F32)) * gate_t.astype(F32)
    ).astype(BF16)
    conv_out = mixed_t.T.reshape(blocks, slab, channels)
    values = project_values(mixed_t, w_value, n_chan)
    attended = attend(queries.reshape(tokens, -1), keys, values, slab)
    return conv_out, attended.reshape(blocks, slab, -1)


def solution(mesh):
    n_chan = mesh.shape["chan"]

    def local(*args):
        return body(n_chan, *args)

    spec = P(None, "seq", "chan")
    return jax.shard_map(
        local,
        mesh=mesh,
        in_specs=(spec, spec, spec, P("chan"), spec, spec, P(None, "chan")),
        out_specs=(spec, spec),
        check_vma=False,
    )
```

```python
import math

import jax
import jax.numpy as jnp
from jax import lax
from jax.experimental import pallas as pl
from jax.experimental.pallas import tpu as pltpu
from jax.sharding import PartitionSpec as P

MESH = pl.DeviceIdType.MESH
F32 = jnp.float32
BF16 = jnp.bfloat16
VM = pltpu.VMEM


def device_at(seq, chan):
    return (jnp.int32(seq), jnp.int32(chan))


def signal(target):
    pl.semaphore_signal(
        pltpu.get_barrier_semaphore(), inc=1, device_id=target, device_id_type=MESH
    )


def remote(src, dst, send, recv, target):
    return pltpu.make_async_remote_copy(
        src_ref=src,
        dst_ref=dst,
        send_sem=send,
        recv_sem=recv,
        device_id=target,
        device_id_type=MESH,
    )


def exchange_kernel(n, along_seq, spread, src, dst, send, recv, own):
    seq = lax.axis_index("seq")
    chan = lax.axis_index("chan")
    me = seq if along_seq else chan

    def peer(step):
        other = lax.rem(me + step, n)
        return other, (device_at(other, chan) if along_seq else device_at(seq, other))

    def greet(step, carry):
        signal(peer(step)[1])
        return carry

    lax.fori_loop(1, n, greet, 0)
    local = pltpu.make_async_copy(src if spread else src.at[me], dst.at[me], own)
    local.start()
    pl.semaphore_wait(pltpu.get_barrier_semaphore(), n - 1)

    def post(step, carry):
        other, target = peer(step)
        remote(
            src if spread else src.at[other], dst.at[me], send.at[step], recv.at[step], target
        ).start()
        return carry

    lax.fori_loop(1, n, post, 0)

    def finish(step, carry):
        other, target = peer(step)
        back = lax.rem(me + n - step, n)
        done = remote(
            src if spread else src.at[other], dst.at[back], send.at[step], recv.at[step], target
        )
        done.wait()
        return carry

    lax.fori_loop(1, n, finish, 0)
    local.wait()


def all_to_all(blocks, collective):
    n = blocks.shape[0]

    def kernel(src, dst, send, recv, own):
        exchange_kernel(n, True, False, src, dst, send, recv, own)

    return pl.pallas_call(
        kernel,
        out_shape=jax.ShapeDtypeStruct(blocks.shape, blocks.dtype),
        in_specs=[pl.BlockSpec(memory_space=VM)],
        out_specs=pl.BlockSpec(memory_space=VM),
        scratch_shapes=[
            pltpu.SemaphoreType.DMA((n,)),
            pltpu.SemaphoreType.DMA((n,)),
            pltpu.SemaphoreType.DMA,
        ],
        compiler_params=pltpu.CompilerParams(collective_id=collective, has_side_effects=True),
    )(blocks)


SIDE = 4
COPIES = 26


class Gather:
    def __init__(self, own_ref, buf, send, recv, own_sem):
        seq = lax.axis_index("seq")
        self.chan = lax.axis_index("chan")
        self.own_ref, self.buf, self.send, self.recv, self.own_sem = (
            own_ref, buf, send, recv, own_sem
        )
        self.core = lax.rem(seq, 2)
        self.x = lax.rem(seq // 2, SIDE)
        self.y = seq // (2 * SIDE)
        self.half = own_ref.shape[0] // 2

    def at(self, y, x, core):
        return device_at((y * SIDE + x) * 2 + core, self.chan)

    def step(self, half, phase, by):
        along_x = (half == 0) == (phase == 1)
        if along_x:
            return self.at(self.y, lax.rem(self.x + by + SIDE, SIDE), self.core)
        return self.at(lax.rem(self.y + by + SIDE, SIDE), self.x, self.core)

    def block(self, half, phase, by):
        rows = pl.ds(half * self.half, self.half)
        along_x = (half == 0) == (phase == 1)
        y, x = self.y, self.x
        if along_x:
            x = lax.rem(x + by + SIDE, SIDE)
        else:
            y = lax.rem(y + by + SIDE, SIDE)
        return y, x, along_x, rows

    def one(self, half, by):
        y, x, _, rows = self.block(half, 1, by)
        return self.buf.at[y, x, self.core, rows]

    def row(self, half, by, core=None, part=None):
        y, x, along_x, rows = self.block(half, 2, by)
        core = self.core if core is None else core
        if part is not None:
            quarter = self.half // 2
            rows = pl.ds(half * self.half + part * quarter, quarter)
        if along_x:
            return self.buf.at[:, x, core, rows]
        return self.buf.at[y, :, core, rows]

    def sems(self, half, number):
        index = half * 13 + number
        return self.send.at[index], self.recv.at[index]

    def greet(self):
        for by in (1, 2, 3):
            signal(self.step(0, 1, by))
            signal(self.step(1, 1, by))
        signal(self.at(self.y, self.x, 1 - self.core))
        return 7


    def first(self, half, i, landing=False):
        by = (1, -1, 2)[i]
        rows = pl.ds(half * self.half, self.half)
        dst = self.one(half, -by) if landing else self.one(half, 0)
        return remote(self.own_ref.at[rows], dst, *self.sems(half, i), self.step(half, 1, by))

    def second(self, half, i, landing=False):
        by = (1, -1)[i]
        dst = self.row(half, -by) if landing else self.row(half, 0)
        return remote(self.row(half, 0), dst, *self.sems(half, 3 + i), self.step(half, 2, by))

    def relay(self, half, i, landing=False):
        by = (1, -1)[i]
        src = self.row(half, -by, part=i)
        dst = self.row(half, 2, part=i) if landing else src
        return remote(src, dst, *self.sems(half, 5 + i), self.step(half, 2, by))

    def across(self, half, i, landing=False):
        by, part = ((0, None), (-1, None), (1, None), (2, 0), (2, 1))[i]
        src = self.row(half, by, part=part)
        dst = self.row(half, by, core=1 - self.core, part=part) if landing else src
        return remote(
            src, dst, *self.sems(half, 7 + i), self.at(self.y, self.x, 1 - self.core)
        )

    def start(self):
        self.local = pltpu.make_async_copy(
            self.own_ref, self.buf.at[self.y, self.x, self.core], self.own_sem
        )
        self.local.start()
        for i in range(3):
            for half in range(2):
                self.first(half, i).start()

    def middle(self):
        self.local.wait()
        for half in range(2):
            for i in range(3):
                self.first(half, i, True).wait_recv()
            for i in range(2):
                self.second(half, i).start()
        for half in range(2):
            self.across(half, 0).start()

    def late(self):
        for i in range(2):
            for half in range(2):
                self.second(half, i, True).wait_recv()
                self.relay(half, i).start()
        for i in range(2):
            for half in range(2):
                self.across(half, 1 + i).start()

    def last(self):
        for i in range(2):
            for half in range(2):
                self.relay(half, i, True).wait_recv()
                self.across(half, 3 + i).start()

    def end(self):
        for half in range(2):
            for i in range(5):
                self.across(half, i, True).wait_recv()
        for half in range(2):
            for i in range(3):
                self.first(half, i).wait_send()
            for i in range(2):
                self.second(half, i).wait_send()
                self.relay(half, i).wait_send()
            for i in range(5):
                self.across(half, i).wait_send()


def gather_scratch():
    return [
        pltpu.SemaphoreType.DMA((COPIES,)),
        pltpu.SemaphoreType.DMA((COPIES,)),
        pltpu.SemaphoreType.DMA,
    ]


TILE = 128
GROUP = 16


def spread_taps(h_ref, base, ch):
    wide = jnp.broadcast_to(h_ref[ch], (8, h_ref.shape[2])).astype(F32)
    sub = lax.broadcasted_iota(jnp.int32, wide.shape, 0)
    for bit in (1, 2, 4):
        wide = jnp.where((sub & bit) != 0, pltpu.roll(wide, bit, 1), wide)
    base[...] = wide


def spread_signal(x_ref, shifted, ch):
    x = x_ref[ch].astype(F32)
    row = lax.broadcasted_iota(jnp.int32, x.shape, 0)
    for k in range(GROUP):
        moved = x if k == 0 else jnp.where(row >= k, pltpu.roll(x, k, 0), 0.0)
        lanes = pl.ds((k % AT_ONCE) * TILE, TILE)
        shifted[k // AT_ONCE, :, lanes] = moved.astype(BF16)


AT_ONCE = 4


def toeplitz(base, lane):
    window = base[:, pl.ds(pl.multiple_of(lane, TILE), (AT_ONCE + 1) * TILE)]
    moved = [window if u == 0 else pltpu.roll(window, 8 * u, 1) for u in range(TILE // 8)]
    parts = []
    for d in range(AT_ONCE):
        parts += [m[:, (d + 1) * TILE : (d + 2) * TILE] for m in moved]
    return jnp.concatenate(parts, axis=0).astype(BF16)


def convolve_group(base, shifted, total, g, blocks):
    rows = blocks - GROUP * g

    def some(kk, acc):
        block = toeplitz(base, (GROUP * g + AT_ONCE * kk) * TILE)
        left = shifted[kk, pl.ds(0, rows), :]
        return acc + jnp.dot(left, block, preferred_element_type=F32)

    acc = lax.fori_loop(0, GROUP // AT_ONCE, some, jnp.zeros((rows, TILE), F32), unroll=2)
    if g == 0:
        total[...] = acc
    else:
        total[pl.ds(GROUP * g, rows), :] += acc


def conv_and_keys(x, h, keys):
    tokens, head = keys.shape

    def kernel(x_ref, h_ref, k_ref, y_ref, buf, base, shifted, total, send, recv, own):
        gather = Gather(k_ref, buf, send, recv, own)
        pl.semaphore_wait(pltpu.get_barrier_semaphore(), gather.greet())
        gather.start()
        stages = {(0, 1): gather.middle, (0, 7): gather.late, (1, 1): gather.last}
        for ch in range(x_ref.shape[0]):
            spread_taps(h_ref, base, ch)
            spread_signal(x_ref, shifted, ch)
            for g in range(x_ref.shape[1] // GROUP):
                convolve_group(base, shifted, total, g, x_ref.shape[1])
                if (ch, g) in stages:
                    stages[ch, g]()
            y_ref[ch] = total[...].astype(BF16)
        gather.end()

    blocks = x.shape[1]
    return pl.pallas_call(
        kernel,
        out_shape=(
            jax.ShapeDtypeStruct(x.shape, BF16),
            jax.ShapeDtypeStruct((SIDE, SIDE, 2, tokens, head), BF16),
        ),
        in_specs=[pl.BlockSpec(memory_space=VM)] * 3,
        out_specs=(pl.BlockSpec(memory_space=VM),) * 2,
        scratch_shapes=[
            pltpu.VMEM((8, h.shape[2]), F32),
            pltpu.VMEM((GROUP // AT_ONCE, blocks, AT_ONCE * TILE), BF16),
            pltpu.VMEM((blocks, TILE), F32),
        ]
        + gather_scratch(),
        compiler_params=pltpu.CompilerParams(collective_id=1, has_side_effects=True),
    )(x, h, keys)


QROWS = 128


def key_block(buf, index, slab):
    part = buf[:, :, :, pl.ds(pl.multiple_of(index * slab, slab), slab), :]
    return part.reshape(2 * SIDE * SIDE * slab, part.shape[-1])


class Ring:
    def __init__(self, n, src, held, send, recv, own):
        self.n, self.src, self.held, self.send, self.recv, self.own = n, src, held, send, recv, own
        self.seq = lax.axis_index("seq")
        self.me = lax.axis_index("chan")
        self.steps = n // 2

    def greet(self):
        signal(device_at(self.seq, lax.rem(self.me + 1, self.n)))
        signal(device_at(self.seq, lax.rem(self.me + self.n - 1, self.n)))
        return 2

    def copy(self, k, side, landing=False):
        way = (1, -1)[side]
        away = k if landing else k - 1
        block = lax.rem(self.me - way * away + self.n, self.n)
        half = self.src.shape[0] // 2
        rows = pl.ds(side * half, half) if k == self.steps else pl.ds(0, 2 * half)
        dst = self.held.at[block, rows]
        src = self.src.at[rows] if k == 1 else dst
        index = 2 * (k - 1) + side
        target = device_at(self.seq, lax.rem(self.me + way + self.n, self.n))
        return remote(src, dst, self.send.at[index], self.recv.at[index], target)

    def start(self, k):
        if k == 1:
            self.local = pltpu.make_async_copy(self.src, self.held.at[self.me], self.own)
            self.local.start()
        for side in range(2):
            if k > 1:
                self.copy(k - 1, side, True).wait_recv()
            self.copy(k, side).start()

    def end(self):
        for side in range(2):
            self.copy(self.steps, side, True).wait_recv()
        self.local.wait()
        for k in range(1, self.steps + 1):
            for side in range(2):
                self.copy(k, side).wait_send()


def attend(queries, keys, mixed, w_value, slab, n_chan):
    tokens, head = queries.shape
    scale = math.log2(math.e) / math.sqrt(head)
    width = 2 * SIDE * SIDE * slab
    per_tile = QROWS // slab
    groups = width // TILE
    pv_blocks = 2

    def kernel(
        q_ref, k_buf, m_ref, w_ref, out, buf, weights, best, totals, acc, held, value,
        send, recv, own, ring_send, ring_recv, ring_own,
    ):
        first_row = lax.axis_index("seq") * slab
        row = lax.broadcasted_iota(jnp.int32, (QROWS, TILE), 0)
        lane = lax.broadcasted_iota(jnp.int32, (QROWS, TILE), 1)
        limit = (row // slab) * width + first_row + row % slab - lane

        def scores(tile, block):
            q = q_ref[pl.ds(tile * QROWS, tokens - tile * QROWS), :]
            return lax.dot_general(
                q, key_block(k_buf, block, slab), (((1,), (1,)), ((), ())),
                preferred_element_type=F32,
            )

        def allowed(tile, block, part):
            return (block - tile * per_tile) * width + part * TILE <= limit

        def edge(tile, block, part, values, other):
            top = jnp.where(allowed(tile, block, part), values[:QROWS], other)
            if values.shape[0] == QROWS:
                return top
            return jnp.concatenate([top, values[QROWS:]], axis=0)

        def find_best(tile, low, high):
            rows = pl.ds(tile * QROWS, tokens - tile * QROWS)

            def one(block, carry):
                s = scores(tile, block)
                top = best[rows, :]
                for part in range(groups):
                    piece = s[:, part * TILE : (part + 1) * TILE]
                    top = jnp.maximum(top, edge(tile, block, part, piece, -1e30))
                best[rows, :] = top
                return carry

            lax.fori_loop(tile * per_tile + low, tile * per_tile + high, one, 0)

        def weigh(tile, low, high):
            rows = pl.ds(tile * QROWS, tokens - tile * QROWS)

            def one(block, carry):
                s = scores(tile, block)
                top = best[rows, :]
                total = totals[rows, :]
                for part in range(groups):
                    piece = s[:, part * TILE : (part + 1) * TILE]
                    w = jnp.exp2((piece - top) * scale)
                    w = edge(tile, block, part, w, 0.0)
                    lanes = pl.ds(pl.multiple_of(block * width + part * TILE, TILE), TILE)
                    weights[rows, lanes] = w.astype(BF16)
                    total = total + w
                totals[rows, :] = total
                return carry

            lax.fori_loop(tile * per_tile + low, tile * per_tile + high, one, 0)

        ring = Ring(n_chan, m_ref, held, ring_send, ring_recv, ring_own)
        gather = Gather(value, buf, send, recv, own)
        greeted = ring.greet() + gather.greet()
        pl.semaphore_wait(pltpu.get_barrier_semaphore(), greeted)

        ring.start(1)
        best[...] = jnp.full(best.shape, -1e30, F32)
        totals[...] = jnp.zeros(totals.shape, F32)
        find_best(0, 0, 4)
        ring.start(2)
        find_best(0, 4, 8)
        ring.start(3)
        find_best(1, 0, 8)
        ring.start(4)
        find_best(2, 0, 8)
        find_best(3, 0, 8)
        best[...] = jnp.broadcast_to(jnp.max(best[...], axis=1, keepdims=True), best.shape)
        ring.end()
        value[...] = lax.dot_general(
            held[...].reshape(held.shape[0] * held.shape[1], tokens),
            w_ref[...],
            (((0,), (0,)), ((), ())),
            preferred_element_type=F32,
        ).astype(BF16)
        weigh(3, 0, 8)
        gather.start()
        weigh(2, 0, 8)
        weigh(1, 0, 4)
        gather.middle()
        weigh(1, 4, 8)
        weigh(0, 0, 4)
        gather.late()
        weigh(0, 4, 8)
        gather.last()
        gather.end()

        acc[...] = jnp.zeros(acc.shape, F32)
        for tile in range(tokens // QROWS):
            rows = pl.ds(tile * QROWS, tokens - tile * QROWS)

            def add(step, carry, rows=rows, tile=tile):
                block = tile * per_tile + step * pv_blocks
                lanes = pl.ds(pl.multiple_of(block * width, width), pv_blocks * width)
                right = jnp.concatenate(
                    [key_block(buf, block + i, slab) for i in range(pv_blocks)], axis=0
                )
                acc[rows, :] += jnp.dot(weights[rows, lanes], right, preferred_element_type=F32)
                return carry

            lax.fori_loop(0, per_tile // pv_blocks, add, 0)
        total = jnp.sum(totals[...], axis=1, keepdims=True)
        out[...] = (acc[...] / total).astype(BF16)

    return pl.pallas_call(
        kernel,
        out_shape=jax.ShapeDtypeStruct((tokens, head), BF16),
        in_specs=[pl.BlockSpec(memory_space=VM)] * 4,
        out_specs=pl.BlockSpec(memory_space=VM),
        scratch_shapes=[
            pltpu.VMEM((SIDE, SIDE, 2, tokens, head), BF16),
            pltpu.VMEM((tokens, tokens * 2 * SIDE * SIDE), BF16),
            pltpu.VMEM((tokens, TILE), F32),
            pltpu.VMEM((tokens, TILE), F32),
            pltpu.VMEM((tokens, head), F32),
            pltpu.VMEM((n_chan,) + mixed.shape, BF16),
            pltpu.VMEM((tokens, head), BF16),
        ]
        + gather_scratch()
        + [
            pltpu.SemaphoreType.DMA((n_chan,)),
            pltpu.SemaphoreType.DMA((n_chan,)),
            pltpu.SemaphoreType.DMA,
        ],
        compiler_params=pltpu.CompilerParams(collective_id=2, has_side_effects=True),
    )(queries, keys, mixed, w_value)


def body(n_chan, conv_in, conv_gate, long_filter, skip_gain, queries, keys_in, w_value):
    blocks, slab, channels = conv_in.shape
    tokens = blocks * slab
    n_seq = 2 * SIDE * SIDE
    each = channels // n_seq
    length = tokens * n_seq
    lines = tokens // TILE
    signal_t = conv_in.reshape(tokens, channels).T
    taps_t = long_filter.reshape(tokens, channels).astype(BF16).T
    packed = jnp.stack(
        [signal_t.reshape(n_seq, each, tokens), taps_t.reshape(n_seq, each, tokens)], axis=1
    ).reshape(n_seq, 2 * each * lines, TILE)
    got = all_to_all(packed, 0)
    whole = (
        got.reshape(n_seq, 2, each, blocks, slab).transpose(1, 2, 3, 0, 4).reshape(2, each, length)
    )
    x = whole[0].reshape(each, length // TILE, TILE)
    h = jnp.pad(whole[1].astype(F32), ((0, 0), (TILE, 0))).reshape(each, 1, length + TILE)
    y, keys = conv_and_keys(x, h, keys_in.reshape(tokens, -1))
    back = (
        y.reshape(each, blocks, n_seq, slab)
        .transpose(2, 0, 1, 3)
        .reshape(n_seq, each * lines, TILE)
    )
    convolved = all_to_all(back, 4).reshape(channels, tokens).astype(F32)
    gate_t = conv_gate.reshape(tokens, channels).T
    mixed_t = (
        (convolved + skip_gain[:, None] * signal_t.astype(F32)) * gate_t.astype(F32)
    ).astype(BF16)
    conv_out = mixed_t.T.reshape(blocks, slab, channels)
    attended = attend(queries.reshape(tokens, -1), keys, mixed_t, w_value, slab, n_chan)
    return conv_out, attended.reshape(blocks, slab, -1)


def solution(mesh):
    n_chan = mesh.shape["chan"]

    def local(*args):
        return body(n_chan, *args)

    spec = P(None, "seq", "chan")
    return jax.shard_map(
        local,
        mesh=mesh,
        in_specs=(spec, spec, spec, P("chan"), spec, spec, P(None, "chan")),
        out_specs=(spec, spec),
        check_vma=False,
    )
```

```python
import math

import jax
import jax.numpy as jnp
from jax import lax
from jax.experimental import pallas as pl
from jax.experimental.pallas import tpu as pltpu
from jax.sharding import PartitionSpec as P

MESH = pl.DeviceIdType.MESH
F32 = jnp.float32
BF16 = jnp.bfloat16
VM = pltpu.VMEM


def device_at(seq, chan):
    return (jnp.int32(seq), jnp.int32(chan))


def signal(target):
    pl.semaphore_signal(
        pltpu.get_barrier_semaphore(), inc=1, device_id=target, device_id_type=MESH
    )


def remote(src, dst, send, recv, target):
    return pltpu.make_async_remote_copy(
        src_ref=src,
        dst_ref=dst,
        send_sem=send,
        recv_sem=recv,
        device_id=target,
        device_id_type=MESH,
    )


def exchange_kernel(n, along_seq, spread, src, dst, send, recv, own):
    seq = lax.axis_index("seq")
    chan = lax.axis_index("chan")
    me = seq if along_seq else chan

    def peer(step):
        other = lax.rem(me + step, n)
        return other, (device_at(other, chan) if along_seq else device_at(seq, other))

    def greet(step, carry):
        signal(peer(step)[1])
        return carry

    lax.fori_loop(1, n, greet, 0)
    local = pltpu.make_async_copy(src if spread else src.at[me], dst.at[me], own)
    local.start()
    pl.semaphore_wait(pltpu.get_barrier_semaphore(), n - 1)

    def post(step, carry):
        other, target = peer(step)
        remote(
            src if spread else src.at[other], dst.at[me], send.at[step], recv.at[step], target
        ).start()
        return carry

    lax.fori_loop(1, n, post, 0)

    def finish(step, carry):
        other, target = peer(step)
        back = lax.rem(me + n - step, n)
        done = remote(
            src if spread else src.at[other], dst.at[back], send.at[step], recv.at[step], target
        )
        done.wait()
        return carry

    lax.fori_loop(1, n, finish, 0)
    local.wait()


def all_to_all(blocks, collective):
    n = blocks.shape[0]

    def kernel(src, dst, send, recv, own):
        exchange_kernel(n, True, False, src, dst, send, recv, own)

    return pl.pallas_call(
        kernel,
        out_shape=jax.ShapeDtypeStruct(blocks.shape, blocks.dtype),
        in_specs=[pl.BlockSpec(memory_space=VM)],
        out_specs=pl.BlockSpec(memory_space=VM),
        scratch_shapes=[
            pltpu.SemaphoreType.DMA((n,)),
            pltpu.SemaphoreType.DMA((n,)),
            pltpu.SemaphoreType.DMA,
        ],
        compiler_params=pltpu.CompilerParams(collective_id=collective, has_side_effects=True),
    )(blocks)


SIDE = 4
COPIES = 28


class Gather:
    def __init__(self, own_ref, buf, send, recv, own_sem):
        seq = lax.axis_index("seq")
        self.chan = lax.axis_index("chan")
        self.own_ref, self.buf, self.send, self.recv, self.own_sem = (
            own_ref, buf, send, recv, own_sem
        )
        self.core = lax.rem(seq, 2)
        self.x = lax.rem(seq // 2, SIDE)
        self.y = seq // (2 * SIDE)
        self.half = own_ref.shape[0] // 2

    def at(self, y, x, core):
        return device_at((y * SIDE + x) * 2 + core, self.chan)

    def step(self, half, phase, by):
        along_x = (half == 0) == (phase == 1)
        if along_x:
            return self.at(self.y, lax.rem(self.x + by + SIDE, SIDE), self.core)
        return self.at(lax.rem(self.y + by + SIDE, SIDE), self.x, self.core)

    def block(self, half, phase, by):
        rows = pl.ds(half * self.half, self.half)
        along_x = (half == 0) == (phase == 1)
        y, x = self.y, self.x
        if along_x:
            x = lax.rem(x + by + SIDE, SIDE)
        else:
            y = lax.rem(y + by + SIDE, SIDE)
        return y, x, along_x, rows

    def one(self, half, by):
        y, x, _, rows = self.block(half, 1, by)
        return self.buf.at[y, x, self.core, rows]

    def row(self, half, by, core=None, part=None):
        y, x, along_x, rows = self.block(half, 2, by)
        core = self.core if core is None else core
        if part is not None:
            quarter = self.half // 2
            rows = pl.ds(half * self.half + part * quarter, quarter)
        if along_x:
            return self.buf.at[:, x, core, rows]
        return self.buf.at[y, :, core, rows]

    def sems(self, half, number):
        index = half * 14 + number
        return self.send.at[index], self.recv.at[index]

    def greet(self):
        for by in (1, 2, 3):
            signal(self.step(0, 1, by))
            signal(self.step(1, 1, by))
        signal(self.at(self.y, self.x, 1 - self.core))
        return 7


    def first(self, half, i, landing=False):
        by = (1, -1, 2)[i]
        rows = pl.ds(half * self.half, self.half)
        dst = self.one(half, -by) if landing else self.one(half, 0)
        return remote(self.own_ref.at[rows], dst, *self.sems(half, i), self.step(half, 1, by))

    def second(self, half, i, part, landing=False):
        by = (1, -1)[i]
        src = self.row(half, 0, part=part)
        dst = self.row(half, -by, part=part) if landing else src
        return remote(src, dst, *self.sems(half, 3 + 2 * i + part), self.step(half, 2, by))

    def relay(self, half, i, landing=False):
        by = (1, -1)[i]
        src = self.row(half, -by, part=i)
        dst = self.row(half, 2, part=i) if landing else src
        return remote(src, dst, *self.sems(half, 7 + i), self.step(half, 2, by))

    def across(self, half, i, landing=False):
        by, part = ((0, None), (-1, None), (1, None), (2, 0), (2, 1))[i]
        src = self.row(half, by, part=part)
        dst = self.row(half, by, core=1 - self.core, part=part) if landing else src
        return remote(
            src, dst, *self.sems(half, 9 + i), self.at(self.y, self.x, 1 - self.core)
        )

    def start(self):
        self.local = pltpu.make_async_copy(
            self.own_ref, self.buf.at[self.y, self.x, self.core], self.own_sem
        )
        self.local.start()
        for i in range(3):
            for half in range(2):
                self.first(half, i).start()

    def middle(self):
        self.local.wait()
        for half in range(2):
            for i in range(3):
                self.first(half, i, True).wait_recv()
            for i in range(2):
                self.second(half, i, i).start()
        for half in range(2):
            for i in range(2):
                self.second(half, i, 1 - i).start()
            self.across(half, 0).start()

    def late(self):
        for i in range(2):
            for half in range(2):
                self.second(half, i, i, True).wait_recv()
                self.relay(half, i).start()

    def last(self):
        for i in range(2):
            for half in range(2):
                self.second(half, i, 1 - i, True).wait_recv()
                self.across(half, 1 + i).start()
        for i in range(2):
            for half in range(2):
                self.relay(half, i, True).wait_recv()
                self.across(half, 3 + i).start()

    def end(self):
        for half in range(2):
            for i in range(5):
                self.across(half, i, True).wait_recv()
        for half in range(2):
            for i in range(3):
                self.first(half, i).wait_send()
            for i in range(2):
                self.second(half, i, 0).wait_send()
                self.second(half, i, 1).wait_send()
                self.relay(half, i).wait_send()
            for i in range(5):
                self.across(half, i).wait_send()


def gather_scratch():
    return [
        pltpu.SemaphoreType.DMA((COPIES,)),
        pltpu.SemaphoreType.DMA((COPIES,)),
        pltpu.SemaphoreType.DMA,
    ]


TILE = 128
GROUP = 16


def spread_taps(h_ref, base, ch):
    wide = jnp.broadcast_to(h_ref[ch], (8, h_ref.shape[2])).astype(F32)
    sub = lax.broadcasted_iota(jnp.int32, wide.shape, 0)
    for bit in (1, 2, 4):
        wide = jnp.where((sub & bit) != 0, pltpu.roll(wide, bit, 1), wide)
    base[...] = wide


def spread_signal(x_ref, shifted, ch):
    x = x_ref[ch].astype(F32)
    row = lax.broadcasted_iota(jnp.int32, x.shape, 0)
    for k in range(GROUP):
        moved = x if k == 0 else jnp.where(row >= k, pltpu.roll(x, k, 0), 0.0)
        lanes = pl.ds((k % AT_ONCE) * TILE, TILE)
        shifted[k // AT_ONCE, :, lanes] = moved.astype(BF16)


AT_ONCE = 4


def toeplitz(base, lane):
    window = base[:, pl.ds(pl.multiple_of(lane, TILE), (AT_ONCE + 1) * TILE)]
    moved = [window if u == 0 else pltpu.roll(window, 8 * u, 1) for u in range(TILE // 8)]
    parts = []
    for d in range(AT_ONCE):
        parts += [m[:, (d + 1) * TILE : (d + 2) * TILE] for m in moved]
    return jnp.concatenate(parts, axis=0).astype(BF16)


def convolve_group(base, shifted, total, g, blocks):
    rows = blocks - GROUP * g

    def some(kk, acc):
        block = toeplitz(base, (GROUP * g + AT_ONCE * kk) * TILE)
        left = shifted[kk, pl.ds(0, rows), :]
        return acc + jnp.dot(left, block, preferred_element_type=F32)

    acc = lax.fori_loop(0, GROUP // AT_ONCE, some, jnp.zeros((rows, TILE), F32), unroll=2)
    if g == 0:
        total[...] = acc
    else:
        total[pl.ds(GROUP * g, rows), :] += acc


def conv_and_keys(x, h, keys):
    tokens, head = keys.shape

    def kernel(x_ref, h_ref, k_ref, y_ref, buf, base, shifted, total, send, recv, own):
        gather = Gather(k_ref, buf, send, recv, own)
        pl.semaphore_wait(pltpu.get_barrier_semaphore(), gather.greet())
        gather.start()
        stages = {(0, 1): gather.middle, (0, 7): gather.late, (1, 1): gather.last}
        for ch in range(x_ref.shape[0]):
            spread_taps(h_ref, base, ch)
            spread_signal(x_ref, shifted, ch)
            for g in range(x_ref.shape[1] // GROUP):
                convolve_group(base, shifted, total, g, x_ref.shape[1])
                if (ch, g) in stages:
                    stages[ch, g]()
            y_ref[ch] = total[...].astype(BF16)
        gather.end()

    blocks = x.shape[1]
    return pl.pallas_call(
        kernel,
        out_shape=(
            jax.ShapeDtypeStruct(x.shape, BF16),
            jax.ShapeDtypeStruct((SIDE, SIDE, 2, tokens, head), BF16),
        ),
        in_specs=[pl.BlockSpec(memory_space=VM)] * 3,
        out_specs=(pl.BlockSpec(memory_space=VM),) * 2,
        scratch_shapes=[
            pltpu.VMEM((8, h.shape[2]), F32),
            pltpu.VMEM((GROUP // AT_ONCE, blocks, AT_ONCE * TILE), BF16),
            pltpu.VMEM((blocks, TILE), F32),
        ]
        + gather_scratch(),
        compiler_params=pltpu.CompilerParams(collective_id=1, has_side_effects=True),
    )(x, h, keys)


QROWS = 128
SLICE = 32
UNROLL = 2


def key_block(buf, index, slab):
    part = buf[:, :, :, pl.ds(pl.multiple_of(index * slab, slab), slab), :]
    return part.reshape(2 * SIDE * SIDE * slab, part.shape[-1])


class Ring:
    def __init__(self, n, src, held, send, recv, own):
        self.n, self.src, self.held, self.send, self.recv, self.own = n, src, held, send, recv, own
        self.seq = lax.axis_index("seq")
        self.me = lax.axis_index("chan")
        self.steps = n // 2

    def greet(self):
        signal(device_at(self.seq, lax.rem(self.me + 1, self.n)))
        signal(device_at(self.seq, lax.rem(self.me + self.n - 1, self.n)))
        return 2

    def copy(self, k, side, landing=False):
        way = (1, -1)[side]
        away = k if landing else k - 1
        block = lax.rem(self.me - way * away + self.n, self.n)
        half = self.src.shape[0] // 2
        rows = pl.ds(side * half, half) if k == self.steps else pl.ds(0, 2 * half)
        dst = self.held.at[block, rows]
        src = self.src.at[rows] if k == 1 else dst
        index = 2 * (k - 1) + side
        target = device_at(self.seq, lax.rem(self.me + way + self.n, self.n))
        return remote(src, dst, self.send.at[index], self.recv.at[index], target)

    def start(self, k):
        if k == 1:
            self.local = pltpu.make_async_copy(self.src, self.held.at[self.me], self.own)
            self.local.start()
        for side in range(2):
            if k > 1:
                self.copy(k - 1, side, True).wait_recv()
            self.copy(k, side).start()

    def end(self):
        for side in range(2):
            self.copy(self.steps, side, True).wait_recv()
        self.local.wait()
        for k in range(1, self.steps + 1):
            for side in range(2):
                self.copy(k, side).wait_send()


def attend(queries, keys, mixed, w_value, slab, n_chan):
    tokens, head = queries.shape
    scale = math.log2(math.e) / math.sqrt(head)
    width = 2 * SIDE * SIDE * slab
    per_tile = QROWS // slab
    groups = width // TILE
    pv_blocks = 2

    def kernel(
        q_ref, k_buf, m_ref, w_ref, out, buf, weights, best, totals, acc, held, value,
        send, recv, own, ring_send, ring_recv, ring_own,
    ):
        first_row = lax.axis_index("seq") * slab
        row = lax.broadcasted_iota(jnp.int32, (QROWS, TILE), 0)
        lane = lax.broadcasted_iota(jnp.int32, (QROWS, TILE), 1)
        limit = (row // slab) * width + first_row + row % slab - lane

        def scores(tile, block):
            q = q_ref[pl.ds(tile * QROWS, tokens - tile * QROWS), :]
            return lax.dot_general(
                q, key_block(k_buf, block, slab), (((1,), (1,)), ((), ())),
                preferred_element_type=F32,
            )

        def allowed(tile, block, part):
            return (block - tile * per_tile) * width + part * TILE <= limit

        def edge(tile, block, part, start, values, other):
            if start >= QROWS:
                return values
            here = allowed(tile, block, part)[start : start + SLICE]
            return jnp.where(here, values, other)

        def find_best(tile, low, high):
            def one(block, carry):
                s = scores(tile, block)
                for start in range(0, s.shape[0], SLICE):
                    rows = pl.ds(tile * QROWS + start, SLICE)
                    top = best[rows, :]
                    for part in range(groups):
                        piece = s[start : start + SLICE, part * TILE : (part + 1) * TILE]
                        top = jnp.maximum(top, edge(tile, block, part, start, piece, -1e30))
                    best[rows, :] = top
                return carry

            lax.fori_loop(tile * per_tile + low, tile * per_tile + high, one, 0, unroll=UNROLL)

        def weigh(tile, low, high):
            def one(block, carry):
                s = scores(tile, block)
                for start in range(0, s.shape[0], SLICE):
                    rows = pl.ds(tile * QROWS + start, SLICE)
                    top = best[rows, :]
                    total = totals[rows, :]
                    for part in range(groups):
                        piece = s[start : start + SLICE, part * TILE : (part + 1) * TILE]
                        w = jnp.exp2((piece - top) * scale)
                        w = edge(tile, block, part, start, w, 0.0)
                        lanes = pl.ds(pl.multiple_of(block * width + part * TILE, TILE), TILE)
                        weights[rows, lanes] = w.astype(BF16)
                        total = total + w
                    totals[rows, :] = total
                return carry

            lax.fori_loop(tile * per_tile + low, tile * per_tile + high, one, 0, unroll=UNROLL)

        ring = Ring(n_chan, m_ref, held, ring_send, ring_recv, ring_own)
        gather = Gather(value, buf, send, recv, own)
        greeted = ring.greet() + gather.greet()
        pl.semaphore_wait(pltpu.get_barrier_semaphore(), greeted)

        ring.start(1)
        best[...] = jnp.full(best.shape, -1e30, F32)
        totals[...] = jnp.zeros(totals.shape, F32)
        find_best(0, 0, 4)
        ring.start(2)
        find_best(0, 4, 8)
        ring.start(3)
        find_best(1, 0, 8)
        ring.start(4)
        find_best(2, 0, 8)
        find_best(3, 0, 8)
        best[...] = jnp.broadcast_to(jnp.max(best[...], axis=1, keepdims=True), best.shape)
        ring.end()
        value[...] = lax.dot_general(
            held[...].reshape(held.shape[0] * held.shape[1], tokens),
            w_ref[...],
            (((0,), (0,)), ((), ())),
            preferred_element_type=F32,
        ).astype(BF16)
        weigh(3, 0, 8)
        gather.start()
        weigh(2, 0, 8)
        weigh(1, 0, 4)
        gather.middle()
        weigh(1, 4, 8)
        weigh(0, 0, 4)
        gather.late()
        weigh(0, 4, 8)
        gather.last()
        gather.end()

        acc[...] = jnp.zeros(acc.shape, F32)
        for tile in range(tokens // QROWS):
            rows = pl.ds(tile * QROWS, tokens - tile * QROWS)

            def add(step, carry, rows=rows, tile=tile):
                block = tile * per_tile + step * pv_blocks
                lanes = pl.ds(pl.multiple_of(block * width, width), pv_blocks * width)
                right = jnp.concatenate(
                    [key_block(buf, block + i, slab) for i in range(pv_blocks)], axis=0
                )
                acc[rows, :] += jnp.dot(weights[rows, lanes], right, preferred_element_type=F32)
                return carry

            lax.fori_loop(0, per_tile // pv_blocks, add, 0, unroll=UNROLL)
        total = jnp.sum(totals[...], axis=1, keepdims=True)
        out[...] = (acc[...] / total).astype(BF16)

    return pl.pallas_call(
        kernel,
        out_shape=jax.ShapeDtypeStruct((tokens, head), BF16),
        in_specs=[pl.BlockSpec(memory_space=VM)] * 4,
        out_specs=pl.BlockSpec(memory_space=VM),
        scratch_shapes=[
            pltpu.VMEM((SIDE, SIDE, 2, tokens, head), BF16),
            pltpu.VMEM((tokens, tokens * 2 * SIDE * SIDE), BF16),
            pltpu.VMEM((tokens, TILE), F32),
            pltpu.VMEM((tokens, TILE), F32),
            pltpu.VMEM((tokens, head), F32),
            pltpu.VMEM((n_chan,) + mixed.shape, BF16),
            pltpu.VMEM((tokens, head), BF16),
        ]
        + gather_scratch()
        + [
            pltpu.SemaphoreType.DMA((n_chan,)),
            pltpu.SemaphoreType.DMA((n_chan,)),
            pltpu.SemaphoreType.DMA,
        ],
        compiler_params=pltpu.CompilerParams(collective_id=2, has_side_effects=True),
    )(queries, keys, mixed, w_value)


def body(n_chan, conv_in, conv_gate, long_filter, skip_gain, queries, keys_in, w_value):
    blocks, slab, channels = conv_in.shape
    tokens = blocks * slab
    n_seq = 2 * SIDE * SIDE
    each = channels // n_seq
    length = tokens * n_seq
    lines = tokens // TILE
    signal_t = conv_in.reshape(tokens, channels).T
    taps_t = long_filter.reshape(tokens, channels).astype(BF16).T
    packed = jnp.stack(
        [signal_t.reshape(n_seq, each, tokens), taps_t.reshape(n_seq, each, tokens)], axis=1
    ).reshape(n_seq, 2 * each * lines, TILE)
    got = all_to_all(packed, 0)
    whole = (
        got.reshape(n_seq, 2, each, blocks, slab).transpose(1, 2, 3, 0, 4).reshape(2, each, length)
    )
    x = whole[0].reshape(each, length // TILE, TILE)
    h = jnp.pad(whole[1].astype(F32), ((0, 0), (TILE, 0))).reshape(each, 1, length + TILE)
    y, keys = conv_and_keys(x, h, keys_in.reshape(tokens, -1))
    back = (
        y.reshape(each, blocks, n_seq, slab)
        .transpose(2, 0, 1, 3)
        .reshape(n_seq, each * lines, TILE)
    )
    convolved = all_to_all(back, 4).reshape(channels, tokens).astype(F32)
    gate_t = conv_gate.reshape(tokens, channels).T
    mixed_t = (
        (convolved + skip_gain[:, None] * signal_t.astype(F32)) * gate_t.astype(F32)
    ).astype(BF16)
    conv_out = mixed_t.T.reshape(blocks, slab, channels)
    attended = attend(queries.reshape(tokens, -1), keys, mixed_t, w_value, slab, n_chan)
    return conv_out, attended.reshape(blocks, slab, -1)


def solution(mesh):
    n_chan = mesh.shape["chan"]

    def local(*args):
        return body(n_chan, *args)

    spec = P(None, "seq", "chan")
    return jax.shard_map(
        local,
        mesh=mesh,
        in_specs=(spec, spec, spec, P("chan"), spec, spec, P(None, "chan")),
        out_specs=(spec, spec),
        check_vma=False,
    )
```

```python
import math

import jax
import jax.numpy as jnp
from jax import lax
from jax.experimental import pallas as pl
from jax.experimental.pallas import tpu as pltpu
from jax.sharding import PartitionSpec as P

MESH = pl.DeviceIdType.MESH
F32 = jnp.float32
BF16 = jnp.bfloat16
VM = pltpu.VMEM


def device_at(seq, chan):
    return (jnp.int32(seq), jnp.int32(chan))


def signal(target):
    pl.semaphore_signal(
        pltpu.get_barrier_semaphore(), inc=1, device_id=target, device_id_type=MESH
    )


def remote(src, dst, send, recv, target):
    return pltpu.make_async_remote_copy(
        src_ref=src,
        dst_ref=dst,
        send_sem=send,
        recv_sem=recv,
        device_id=target,
        device_id_type=MESH,
    )


def exchange_kernel(n, src, dst, send, recv, own, beside=None):
    seq = lax.axis_index("seq")
    chan = lax.axis_index("chan")
    me = seq

    def peer(step):
        other = lax.rem(me + step, n)
        return other, device_at(other, chan)

    def greet(step, carry):
        signal(peer(step)[1])
        return carry

    lax.fori_loop(1, n, greet, 0)
    local = pltpu.make_async_copy(src.at[me], dst.at[me], own)
    local.start()
    pl.semaphore_wait(pltpu.get_barrier_semaphore(), n - 1)

    def post(step, carry):
        other, target = peer(step)
        remote(src.at[other], dst.at[me], send.at[step], recv.at[step], target).start()
        return carry

    lax.fori_loop(1, n, post, 0)
    if beside is not None:
        beside.start()

    def finish(step, carry):
        other, target = peer(step)
        back = lax.rem(me + n - step, n)
        remote(src.at[other], dst.at[back], send.at[step], recv.at[step], target).wait()
        return carry

    lax.fori_loop(1, n, finish, 0)
    local.wait()
    if beside is not None:
        beside.end()


def exchange_scratch(n):
    return [
        pltpu.SemaphoreType.DMA((n,)),
        pltpu.SemaphoreType.DMA((n,)),
        pltpu.SemaphoreType.DMA,
    ]


def all_to_all(blocks, collective):
    n = blocks.shape[0]

    def kernel(src, dst, send, recv, own):
        exchange_kernel(n, src, dst, send, recv, own)

    return pl.pallas_call(
        kernel,
        out_shape=jax.ShapeDtypeStruct(blocks.shape, blocks.dtype),
        in_specs=[pl.BlockSpec(memory_space=VM)],
        out_specs=pl.BlockSpec(memory_space=VM),
        scratch_shapes=exchange_scratch(n),
        compiler_params=pltpu.CompilerParams(collective_id=collective, has_side_effects=True),
    )(blocks)


def exchange_and_rows(blocks, keys):
    n = blocks.shape[0]
    tokens, head = keys.shape

    def kernel(src, k_ref, dst, rows, send, recv, own, row_send, row_recv, row_own):
        beside = FirstRows(k_ref, rows, row_send, row_recv, row_own)
        exchange_kernel(n, src, dst, send, recv, own, beside)

    return pl.pallas_call(
        kernel,
        out_shape=(
            jax.ShapeDtypeStruct(blocks.shape, blocks.dtype),
            jax.ShapeDtypeStruct((2, SIDE, tokens // 2, head), BF16),
        ),
        in_specs=[pl.BlockSpec(memory_space=VM)] * 2,
        out_specs=(pl.BlockSpec(memory_space=VM),) * 2,
        scratch_shapes=exchange_scratch(n)
        + [
            pltpu.SemaphoreType.DMA((6,)),
            pltpu.SemaphoreType.DMA((6,)),
            pltpu.SemaphoreType.DMA((2,)),
        ],
        compiler_params=pltpu.CompilerParams(collective_id=0, has_side_effects=True),
    )(blocks, keys)


SIDE = 4
COPIES = 28


class Gather:
    def __init__(self, own_ref, buf, send, recv, own_sem, rows=None):
        seq = lax.axis_index("seq")
        self.rows = rows
        self.chan = lax.axis_index("chan")
        self.own_ref, self.buf, self.send, self.recv, self.own_sem = (
            own_ref, buf, send, recv, own_sem
        )
        self.core = lax.rem(seq, 2)
        self.x = lax.rem(seq // 2, SIDE)
        self.y = seq // (2 * SIDE)
        self.half = buf.shape[3] // 2

    def at(self, y, x, core):
        return device_at((y * SIDE + x) * 2 + core, self.chan)

    def step(self, half, phase, by):
        along_x = (half == 0) == (phase == 1)
        if along_x:
            return self.at(self.y, lax.rem(self.x + by + SIDE, SIDE), self.core)
        return self.at(lax.rem(self.y + by + SIDE, SIDE), self.x, self.core)

    def block(self, half, phase, by):
        rows = pl.ds(half * self.half, self.half)
        along_x = (half == 0) == (phase == 1)
        y, x = self.y, self.x
        if along_x:
            x = lax.rem(x + by + SIDE, SIDE)
        else:
            y = lax.rem(y + by + SIDE, SIDE)
        return y, x, along_x, rows

    def one(self, half, by):
        y, x, _, rows = self.block(half, 1, by)
        return self.buf.at[y, x, self.core, rows]

    def row(self, half, by, core=None, part=None):
        y, x, along_x, rows = self.block(half, 2, by)
        core = self.core if core is None else core
        if part is not None:
            quarter = self.half // 2
            rows = pl.ds(half * self.half + part * quarter, quarter)
        if along_x:
            return self.buf.at[:, x, core, rows]
        return self.buf.at[y, :, core, rows]

    def sems(self, half, number):
        index = half * 14 + number
        return self.send.at[index], self.recv.at[index]

    def held(self, half, part=None):
        if self.rows is None:
            return self.row(half, 0, part=part)
        if part is None:
            return self.rows.at[half]
        return self.rows.at[half, :, pl.ds(part * (self.half // 2), self.half // 2)]

    def greet(self):
        places = (1, 2, 3) if self.rows is None else (1, 3)
        for by in places:
            signal(self.step(0, 1, by))
            signal(self.step(1, 1, by))
        signal(self.at(self.y, self.x, 1 - self.core))
        return 2 * len(places) + 1


    def first(self, half, i, landing=False):
        by = (1, -1, 2)[i]
        rows = pl.ds(half * self.half, self.half)
        dst = self.one(half, -by) if landing else self.one(half, 0)
        return remote(self.own_ref.at[rows], dst, *self.sems(half, i), self.step(half, 1, by))

    def second(self, half, i, part, landing=False):
        by = (1, -1)[i]
        dst = self.row(half, -by if landing else 0, part=part)
        return remote(self.held(half, part), dst, *self.sems(half, 3 + 2 * i + part), self.step(half, 2, by))

    def relay(self, half, i, landing=False):
        by = (1, -1)[i]
        src = self.row(half, -by, part=i)
        dst = self.row(half, 2, part=i) if landing else src
        return remote(src, dst, *self.sems(half, 7 + i), self.step(half, 2, by))

    def across(self, half, i, landing=False):
        by, part = ((0, None), (-1, None), (1, None), (2, 0), (2, 1))[i]
        src = self.held(half) if i == 0 else self.row(half, by, part=part)
        dst = self.row(half, by, core=1 - self.core if landing else self.core, part=part)
        return remote(
            src, dst, *self.sems(half, 9 + i), self.at(self.y, self.x, 1 - self.core)
        )

    def start(self):
        if self.rows is not None:
            self.local = [
                pltpu.make_async_copy(self.held(half), self.row(half, 0), self.own_sem.at[half])
                for half in range(2)
            ]
            for copy in self.local:
                copy.start()
            self.post()
            return
        copy = pltpu.make_async_copy(
            self.own_ref, self.buf.at[self.y, self.x, self.core], self.own_sem.at[0]
        )
        copy.start()
        self.local = [copy]
        for i in range(3):
            for half in range(2):
                self.first(half, i).start()

    def middle(self):
        self.local.pop().wait()
        for half in range(2):
            for i in range(3):
                self.first(half, i, True).wait_recv()
        self.post()

    def post(self):
        for half in range(2):
            for i in range(2):
                self.second(half, i, i).start()
        for half in range(2):
            for i in range(2):
                self.second(half, i, 1 - i).start()
            self.across(half, 0).start()

    def late(self):
        for half in range(2):
            for i in range(2):
                self.second(half, i, i, True).wait_recv()
                self.relay(half, i).start()

    def last(self):
        for half in range(2):
            for i in range(2):
                self.second(half, i, 1 - i, True).wait_recv()
                self.across(half, 1 + i).start()
        for half in range(2):
            for i in range(2):
                self.relay(half, i, True).wait_recv()
                self.across(half, 3 + i).start()

    def arrived(self, half):
        for i in range(5):
            self.across(half, i, True).wait_recv()

    def end(self):
        for copy in self.local:
            copy.wait()
        for half in range(2):
            for i in range(3):
                if self.rows is None:
                    self.first(half, i).wait_send()
            for i in range(2):
                self.second(half, i, 0).wait_send()
                self.second(half, i, 1).wait_send()
                self.relay(half, i).wait_send()
            for i in range(5):
                self.across(half, i).wait_send()


class FirstRows(Gather):
    def __init__(self, own_ref, rows, send, recv, own_sem):
        seq = lax.axis_index("seq")
        self.chan = lax.axis_index("chan")
        self.own_ref, self.rows, self.send, self.recv, self.own_sem = (
            own_ref, rows, send, recv, own_sem
        )
        self.core = lax.rem(seq, 2)
        self.x = lax.rem(seq // 2, SIDE)
        self.y = seq // (2 * SIDE)
        self.half = own_ref.shape[0] // 2

    def first(self, half, i, landing=False):
        by = (1, -1, 2)[i]
        place = self.x if half == 0 else self.y
        if landing:
            place = lax.rem(place - by + SIDE, SIDE)
        src = self.own_ref.at[pl.ds(half * self.half, self.half)]
        index = half * 3 + i
        return remote(
            src, self.rows.at[half, place], self.send.at[index], self.recv.at[index],
            self.step(half, 1, by),
        )

    def local(self, half):
        src = self.own_ref.at[pl.ds(half * self.half, self.half)]
        place = self.x if half == 0 else self.y
        return pltpu.make_async_copy(src, self.rows.at[half, place], self.own_sem.at[half])

    def start(self):
        for half in range(2):
            for i in range(3):
                self.first(half, i).start()
            self.local(half).start()

    def end(self):
        for half in range(2):
            for i in range(3):
                self.first(half, i, True).wait()
            self.local(half).wait()


def gather_scratch():
    return [
        pltpu.SemaphoreType.DMA((COPIES,)),
        pltpu.SemaphoreType.DMA((COPIES,)),
        pltpu.SemaphoreType.DMA((2,)),
    ]


TILE = 128
GROUP = 16


def spread_taps(h_ref, base, ch):
    wide = jnp.broadcast_to(h_ref[ch], (8, h_ref.shape[2])).astype(F32)
    sub = lax.broadcasted_iota(jnp.int32, wide.shape, 0)
    for bit in (1, 2, 4):
        wide = jnp.where((sub & bit) != 0, pltpu.roll(wide, bit, 1), wide)
    base[...] = wide


def spread_signal(x_ref, shifted, ch):
    x = x_ref[ch].astype(F32)
    row = lax.broadcasted_iota(jnp.int32, x.shape, 0)
    for k in range(GROUP):
        moved = x if k == 0 else jnp.where(row >= k, pltpu.roll(x, k, 0), 0.0)
        lanes = pl.ds((k % AT_ONCE) * TILE, TILE)
        shifted[k // AT_ONCE, :, lanes] = moved.astype(BF16)


AT_ONCE = 4


def toeplitz(base, lane):
    window = base[:, pl.ds(pl.multiple_of(lane, TILE), (AT_ONCE + 1) * TILE)]
    moved = [window if u == 0 else pltpu.roll(window, 8 * u, 1) for u in range(TILE // 8)]
    parts = []
    for d in range(AT_ONCE):
        parts += [m[:, (d + 1) * TILE : (d + 2) * TILE] for m in moved]
    return jnp.concatenate(parts, axis=0).astype(BF16)


def convolve_group(base, shifted, total, g, blocks):
    rows = blocks - GROUP * g

    def some(kk, acc):
        block = toeplitz(base, (GROUP * g + AT_ONCE * kk) * TILE)
        left = shifted[kk, pl.ds(0, rows), :]
        return acc + jnp.dot(left, block, preferred_element_type=F32)

    acc = lax.fori_loop(0, GROUP // AT_ONCE, some, jnp.zeros((rows, TILE), F32), unroll=2)
    if g == 0:
        total[...] = acc
    else:
        total[pl.ds(GROUP * g, rows), :] += acc


def conv_and_keys(x, h, rows):
    tokens, head = 2 * rows.shape[2], rows.shape[3]

    def kernel(x_ref, h_ref, k_ref, y_ref, buf, base, shifted, total, send, recv, own):
        gather = Gather(None, buf, send, recv, own, k_ref)
        pl.semaphore_wait(pltpu.get_barrier_semaphore(), gather.greet())
        gather.start()
        stages = {(0, 3): gather.late, (1, 0): gather.last}
        for ch in range(x_ref.shape[0]):
            spread_taps(h_ref, base, ch)
            spread_signal(x_ref, shifted, ch)
            for g in range(x_ref.shape[1] // GROUP):
                convolve_group(base, shifted, total, g, x_ref.shape[1])
                if (ch, g) in stages:
                    stages[ch, g]()
            y_ref[ch] = total[...].astype(BF16)
        for half in range(2):
            gather.arrived(half)
        gather.end()

    blocks = x.shape[1]
    return pl.pallas_call(
        kernel,
        out_shape=(
            jax.ShapeDtypeStruct(x.shape, BF16),
            jax.ShapeDtypeStruct((SIDE, SIDE, 2, tokens, head), BF16),
        ),
        in_specs=[pl.BlockSpec(memory_space=VM)] * 3,
        out_specs=(pl.BlockSpec(memory_space=VM),) * 2,
        scratch_shapes=[
            pltpu.VMEM((8, h.shape[2]), F32),
            pltpu.VMEM((GROUP // AT_ONCE, blocks, AT_ONCE * TILE), BF16),
            pltpu.VMEM((blocks, TILE), F32),
        ]
        + gather_scratch(),
        compiler_params=pltpu.CompilerParams(collective_id=1, has_side_effects=True),
    )(x, h, rows)


QROWS = 128
SLICE = 32
UNROLL = 2


def key_block(buf, index, slab):
    part = buf[:, :, :, pl.ds(pl.multiple_of(index * slab, slab), slab), :]
    return part.reshape(2 * SIDE * SIDE * slab, part.shape[-1])


class Ring:
    def __init__(self, n, src, held, send, recv, own):
        self.n, self.src, self.held, self.send, self.recv, self.own = n, src, held, send, recv, own
        self.seq = lax.axis_index("seq")
        self.me = lax.axis_index("chan")
        self.steps = n // 2

    def greet(self):
        signal(device_at(self.seq, lax.rem(self.me + 1, self.n)))
        signal(device_at(self.seq, lax.rem(self.me + self.n - 1, self.n)))
        return 2

    def copy(self, k, side, landing=False):
        way = (1, -1)[side]
        away = k if landing else k - 1
        block = lax.rem(self.me - way * away + self.n, self.n)
        half = self.src.shape[0] // 2
        rows = pl.ds(side * half, half) if k == self.steps else pl.ds(0, 2 * half)
        dst = self.held.at[block, rows]
        src = self.src.at[rows] if k == 1 else dst
        index = 2 * (k - 1) + side
        target = device_at(self.seq, lax.rem(self.me + way + self.n, self.n))
        return remote(src, dst, self.send.at[index], self.recv.at[index], target)

    def start(self, k):
        if k == 1:
            self.local = pltpu.make_async_copy(self.src, self.held.at[self.me], self.own)
            self.local.start()
        for side in range(2):
            if k > 1:
                self.copy(k - 1, side, True).wait_recv()
            self.copy(k, side).start()

    def end(self):
        for side in range(2):
            self.copy(self.steps, side, True).wait_recv()
        self.local.wait()
        for k in range(1, self.steps + 1):
            for side in range(2):
                self.copy(k, side).wait_send()


def attend(queries, keys, mixed, w_value, slab, n_chan):
    tokens, head = queries.shape
    scale = math.log2(math.e) / math.sqrt(head)
    width = 2 * SIDE * SIDE * slab
    per_tile = QROWS // slab
    groups = width // TILE
    pv_blocks = 2

    def kernel(
        q_ref, k_buf, m_ref, w_ref, out, buf, weights, best, totals, acc, held, value,
        send, recv, own, ring_send, ring_recv, ring_own,
    ):
        first_row = lax.axis_index("seq") * slab
        row = lax.broadcasted_iota(jnp.int32, (QROWS, TILE), 0)
        lane = lax.broadcasted_iota(jnp.int32, (QROWS, TILE), 1)
        limit = (row // slab) * width + first_row + row % slab - lane

        def scores(tile, block):
            q = q_ref[pl.ds(tile * QROWS, tokens - tile * QROWS), :]
            return lax.dot_general(
                q, key_block(k_buf, block, slab), (((1,), (1,)), ((), ())),
                preferred_element_type=F32,
            )

        def allowed(tile, block, part):
            return (block - tile * per_tile) * width + part * TILE <= limit

        def edge(tile, block, part, start, values, other):
            if start >= QROWS:
                return values
            here = allowed(tile, block, part)[start : start + SLICE]
            return jnp.where(here, values, other)

        def find_best(tile, low, high):
            def one(block, carry):
                s = scores(tile, block)
                for start in range(0, s.shape[0], SLICE):
                    rows = pl.ds(tile * QROWS + start, SLICE)
                    top = best[rows, :]
                    for part in range(groups):
                        piece = s[start : start + SLICE, part * TILE : (part + 1) * TILE]
                        top = jnp.maximum(top, edge(tile, block, part, start, piece, -1e30))
                    best[rows, :] = top
                return carry

            lax.fori_loop(tile * per_tile + low, tile * per_tile + high, one, 0, unroll=UNROLL)

        def weigh(tile, low, high):
            def one(block, carry):
                s = scores(tile, block)
                for start in range(0, s.shape[0], SLICE):
                    rows = pl.ds(tile * QROWS + start, SLICE)
                    top = best[rows, :]
                    total = totals[rows, :]
                    for part in range(groups):
                        piece = s[start : start + SLICE, part * TILE : (part + 1) * TILE]
                        w = jnp.exp2((piece - top) * scale)
                        w = edge(tile, block, part, start, w, 0.0)
                        lanes = pl.ds(pl.multiple_of(block * width + part * TILE, TILE), TILE)
                        weights[rows, lanes] = w.astype(BF16)
                        total = total + w
                    totals[rows, :] = total
                return carry

            lax.fori_loop(tile * per_tile + low, tile * per_tile + high, one, 0, unroll=UNROLL)

        ring = Ring(n_chan, m_ref, held, ring_send, ring_recv, ring_own)
        gather = Gather(value, buf, send, recv, own)
        greeted = ring.greet() + gather.greet()
        pl.semaphore_wait(pltpu.get_barrier_semaphore(), greeted)

        ring.start(1)
        best[...] = jnp.full(best.shape, -1e30, F32)
        totals[...] = jnp.zeros(totals.shape, F32)
        find_best(0, 0, 4)
        ring.start(2)
        find_best(0, 4, 8)
        ring.start(3)
        find_best(1, 0, 8)
        ring.start(4)
        find_best(2, 0, 8)
        find_best(3, 0, 8)
        best[...] = jnp.broadcast_to(jnp.max(best[...], axis=1, keepdims=True), best.shape)
        ring.end()
        value[...] = lax.dot_general(
            held[...].reshape(held.shape[0] * held.shape[1], tokens),
            w_ref[...],
            (((0,), (0,)), ((), ())),
            preferred_element_type=F32,
        ).astype(BF16)
        weigh(3, 0, 8)
        gather.start()
        weigh(2, 0, 8)
        weigh(1, 0, 4)
        gather.middle()
        weigh(1, 4, 8)
        weigh(0, 0, 4)
        gather.late()
        weigh(0, 4, 8)
        acc[...] = jnp.zeros(acc.shape, F32)
        gather.last()
        for tile in range(tokens // QROWS):
            if tile == 0:
                gather.arrived(0)
            if 2 * tile * QROWS == tokens:
                gather.arrived(1)
            rows = pl.ds(tile * QROWS, tokens - tile * QROWS)

            def add(step, carry, rows=rows, tile=tile):
                block = tile * per_tile + step * pv_blocks
                lanes = pl.ds(pl.multiple_of(block * width, width), pv_blocks * width)
                right = jnp.concatenate(
                    [key_block(buf, block + i, slab) for i in range(pv_blocks)], axis=0
                )
                acc[rows, :] += jnp.dot(weights[rows, lanes], right, preferred_element_type=F32)
                return carry

            lax.fori_loop(0, per_tile // pv_blocks, add, 0, unroll=UNROLL)
        gather.end()
        total = jnp.sum(totals[...], axis=1, keepdims=True)
        out[...] = (acc[...] / total).astype(BF16)

    return pl.pallas_call(
        kernel,
        out_shape=jax.ShapeDtypeStruct((tokens, head), BF16),
        in_specs=[pl.BlockSpec(memory_space=VM)] * 4,
        out_specs=pl.BlockSpec(memory_space=VM),
        scratch_shapes=[
            pltpu.VMEM((SIDE, SIDE, 2, tokens, head), BF16),
            pltpu.VMEM((tokens, tokens * 2 * SIDE * SIDE), BF16),
            pltpu.VMEM((tokens, TILE), F32),
            pltpu.VMEM((tokens, TILE), F32),
            pltpu.VMEM((tokens, head), F32),
            pltpu.VMEM((n_chan,) + mixed.shape, BF16),
            pltpu.VMEM((tokens, head), BF16),
        ]
        + gather_scratch()
        + [
            pltpu.SemaphoreType.DMA((n_chan,)),
            pltpu.SemaphoreType.DMA((n_chan,)),
            pltpu.SemaphoreType.DMA,
        ],
        compiler_params=pltpu.CompilerParams(collective_id=2, has_side_effects=True),
    )(queries, keys, mixed, w_value)


def body(n_chan, conv_in, conv_gate, long_filter, skip_gain, queries, keys_in, w_value):
    blocks, slab, channels = conv_in.shape
    tokens = blocks * slab
    n_seq = 2 * SIDE * SIDE
    each = channels // n_seq
    length = tokens * n_seq
    lines = tokens // TILE
    signal_t = conv_in.reshape(tokens, channels).T
    taps_t = long_filter.reshape(tokens, channels).astype(BF16).T
    packed = jnp.stack(
        [signal_t.reshape(n_seq, each, tokens), taps_t.reshape(n_seq, each, tokens)], axis=1
    ).reshape(n_seq, 2 * each * lines, TILE)
    got, rows = exchange_and_rows(packed, keys_in.reshape(tokens, -1))
    whole = (
        got.reshape(n_seq, 2, each, blocks, slab).transpose(1, 2, 3, 0, 4).reshape(2, each, length)
    )
    x = whole[0].reshape(each, length // TILE, TILE)
    h = jnp.pad(whole[1].astype(F32), ((0, 0), (TILE, 0))).reshape(each, 1, length + TILE)
    y, keys = conv_and_keys(x, h, rows)
    back = (
        y.reshape(each, blocks, n_seq, slab)
        .transpose(2, 0, 1, 3)
        .reshape(n_seq, each * lines, TILE)
    )
    convolved = all_to_all(back, 4).reshape(channels, tokens).astype(F32)
    gate_t = conv_gate.reshape(tokens, channels).T
    mixed_t = (
        (convolved + skip_gain[:, None] * signal_t.astype(F32)) * gate_t.astype(F32)
    ).astype(BF16)
    conv_out = mixed_t.T.reshape(blocks, slab, channels)
    attended = attend(queries.reshape(tokens, -1), keys, mixed_t, w_value, slab, n_chan)
    return conv_out, attended.reshape(blocks, slab, -1)


def solution(mesh):
    n_chan = mesh.shape["chan"]

    def local(*args):
        return body(n_chan, *args)

    spec = P(None, "seq", "chan")
    return jax.shard_map(
        local,
        mesh=mesh,
        in_specs=(spec, spec, spec, P("chan"), spec, spec, P(None, "chan")),
        out_specs=(spec, spec),
        check_vma=False,
    )
```

```python
import math

import jax
import jax.numpy as jnp
from jax import lax
from jax.experimental import pallas as pl
from jax.experimental.pallas import tpu as pltpu
from jax.sharding import PartitionSpec as P

MESH = pl.DeviceIdType.MESH
F32 = jnp.float32
BF16 = jnp.bfloat16
VM = pltpu.VMEM


def device_at(seq, chan):
    return (jnp.int32(seq), jnp.int32(chan))


def signal(target):
    pl.semaphore_signal(
        pltpu.get_barrier_semaphore(), inc=1, device_id=target, device_id_type=MESH
    )


def remote(src, dst, send, recv, target):
    return pltpu.make_async_remote_copy(
        src_ref=src,
        dst_ref=dst,
        send_sem=send,
        recv_sem=recv,
        device_id=target,
        device_id_type=MESH,
    )


def exchange_kernel(n, src, dst, send, recv, own, beside=None):
    seq = lax.axis_index("seq")
    chan = lax.axis_index("chan")
    me = seq

    def peer(step):
        other = lax.rem(me + step, n)
        return other, device_at(other, chan)

    def greet(step, carry):
        signal(peer(step)[1])
        return carry

    lax.fori_loop(1, n, greet, 0)
    local = pltpu.make_async_copy(src.at[me], dst.at[me], own)
    local.start()
    pl.semaphore_wait(pltpu.get_barrier_semaphore(), n - 1)

    def post(step, carry):
        other, target = peer(step)
        remote(src.at[other], dst.at[me], send.at[step], recv.at[step], target).start()
        return carry

    lax.fori_loop(1, n, post, 0)
    if beside is not None:
        beside.start()

    def finish(step, carry):
        other, target = peer(step)
        back = lax.rem(me + n - step, n)
        remote(src.at[other], dst.at[back], send.at[step], recv.at[step], target).wait()
        return carry

    lax.fori_loop(1, n, finish, 0)
    local.wait()
    if beside is not None:
        beside.end()


def exchange_scratch(n):
    return [
        pltpu.SemaphoreType.DMA((n,)),
        pltpu.SemaphoreType.DMA((n,)),
        pltpu.SemaphoreType.DMA,
    ]


def all_to_all(blocks, collective):
    n = blocks.shape[0]

    def kernel(src, dst, send, recv, own):
        exchange_kernel(n, src, dst, send, recv, own)

    return pl.pallas_call(
        kernel,
        out_shape=jax.ShapeDtypeStruct(blocks.shape, blocks.dtype),
        in_specs=[pl.BlockSpec(memory_space=VM)],
        out_specs=pl.BlockSpec(memory_space=VM),
        scratch_shapes=exchange_scratch(n),
        compiler_params=pltpu.CompilerParams(collective_id=collective, has_side_effects=True),
    )(blocks)


def exchange_and_rows(blocks, keys):
    n = blocks.shape[0]
    tokens, head = keys.shape

    def kernel(src, k_ref, dst, rows, send, recv, own, row_send, row_recv, row_own):
        beside = FirstRows(k_ref, rows, row_send, row_recv, row_own)
        exchange_kernel(n, src, dst, send, recv, own, beside)

    return pl.pallas_call(
        kernel,
        out_shape=(
            jax.ShapeDtypeStruct(blocks.shape, blocks.dtype),
            jax.ShapeDtypeStruct((2, SIDE, tokens // 2, head), BF16),
        ),
        in_specs=[pl.BlockSpec(memory_space=VM)] * 2,
        out_specs=(pl.BlockSpec(memory_space=VM),) * 2,
        scratch_shapes=exchange_scratch(n)
        + [
            pltpu.SemaphoreType.DMA((6,)),
            pltpu.SemaphoreType.DMA((6,)),
            pltpu.SemaphoreType.DMA((2,)),
        ],
        compiler_params=pltpu.CompilerParams(collective_id=0, has_side_effects=True),
    )(blocks, keys)


SIDE = 4
COPIES = 28


class Gather:
    def __init__(self, own_ref, buf, send, recv, own_sem, rows=None):
        seq = lax.axis_index("seq")
        self.rows = rows
        self.chan = lax.axis_index("chan")
        self.own_ref, self.buf, self.send, self.recv, self.own_sem = (
            own_ref, buf, send, recv, own_sem
        )
        self.core = lax.rem(seq, 2)
        self.x = lax.rem(seq // 2, SIDE)
        self.y = seq // (2 * SIDE)
        self.half = buf.shape[3] // 2

    def at(self, y, x, core):
        return device_at((y * SIDE + x) * 2 + core, self.chan)

    def step(self, half, phase, by):
        along_x = (half == 0) == (phase == 1)
        if along_x:
            return self.at(self.y, lax.rem(self.x + by + SIDE, SIDE), self.core)
        return self.at(lax.rem(self.y + by + SIDE, SIDE), self.x, self.core)

    def block(self, half, phase, by):
        rows = pl.ds(half * self.half, self.half)
        along_x = (half == 0) == (phase == 1)
        y, x = self.y, self.x
        if along_x:
            x = lax.rem(x + by + SIDE, SIDE)
        else:
            y = lax.rem(y + by + SIDE, SIDE)
        return y, x, along_x, rows

    def one(self, half, by):
        y, x, _, rows = self.block(half, 1, by)
        return self.buf.at[y, x, self.core, rows]

    def row(self, half, by, core=None, part=None):
        y, x, along_x, rows = self.block(half, 2, by)
        core = self.core if core is None else core
        if part is not None:
            quarter = self.half // 2
            rows = pl.ds(half * self.half + part * quarter, quarter)
        if along_x:
            return self.buf.at[:, x, core, rows]
        return self.buf.at[y, :, core, rows]

    def sems(self, half, number):
        index = half * 14 + number
        return self.send.at[index], self.recv.at[index]

    def held(self, half, part=None):
        if self.rows is None:
            return self.row(half, 0, part=part)
        if part is None:
            return self.rows.at[half]
        return self.rows.at[half, :, pl.ds(part * (self.half // 2), self.half // 2)]

    def greet(self):
        places = (1, 2, 3) if self.rows is None else (1, 3)
        for by in places:
            signal(self.step(0, 1, by))
            signal(self.step(1, 1, by))
        signal(self.at(self.y, self.x, 1 - self.core))
        return 2 * len(places) + 1


    def first(self, half, i, landing=False):
        by = (1, -1, 2)[i]
        rows = pl.ds(half * self.half, self.half)
        dst = self.one(half, -by) if landing else self.one(half, 0)
        return remote(self.own_ref.at[rows], dst, *self.sems(half, i), self.step(half, 1, by))

    def second(self, half, i, part, landing=False):
        by = (1, -1)[i]
        dst = self.row(half, -by if landing else 0, part=part)
        return remote(self.held(half, part), dst, *self.sems(half, 3 + 2 * i + part), self.step(half, 2, by))

    def relay(self, half, i, landing=False):
        by = (1, -1)[i]
        src = self.row(half, -by, part=i)
        dst = self.row(half, 2, part=i) if landing else src
        return remote(src, dst, *self.sems(half, 7 + i), self.step(half, 2, by))

    def across(self, half, i, landing=False):
        by, part = ((0, None), (-1, None), (1, None), (2, 0), (2, 1))[i]
        src = self.held(half) if i == 0 else self.row(half, by, part=part)
        dst = self.row(half, by, core=1 - self.core if landing else self.core, part=part)
        return remote(
            src, dst, *self.sems(half, 9 + i), self.at(self.y, self.x, 1 - self.core)
        )

    def start(self):
        if self.rows is not None:
            self.local = [
                pltpu.make_async_copy(self.held(half), self.row(half, 0), self.own_sem.at[half])
                for half in range(2)
            ]
            for copy in self.local:
                copy.start()
            self.post()
            return
        copy = pltpu.make_async_copy(
            self.own_ref, self.buf.at[self.y, self.x, self.core], self.own_sem.at[0]
        )
        copy.start()
        self.local = [copy]
        for i in range(3):
            for half in range(2):
                self.first(half, i).start()

    def middle(self):
        self.local.pop().wait()
        for half in range(2):
            for i in range(3):
                self.first(half, i, True).wait_recv()
        self.post()

    def post(self):
        for half in range(2):
            for i in range(2):
                self.second(half, i, i).start()
        for half in range(2):
            for i in range(2):
                self.second(half, i, 1 - i).start()
            self.across(half, 0).start()

    def late(self):
        for half in range(2):
            for i in range(2):
                self.second(half, i, i, True).wait_recv()
                self.relay(half, i).start()

    def last(self):
        for half in range(2):
            for i in range(2):
                self.second(half, i, 1 - i, True).wait_recv()
                self.across(half, 1 + i).start()
        for half in range(2):
            for i in range(2):
                self.relay(half, i, True).wait_recv()
                self.across(half, 3 + i).start()

    def arrived(self, half):
        for i in range(5):
            self.across(half, i, True).wait_recv()

    def placed(self):
        while self.local:
            self.local.pop().wait()

    def end(self):
        self.placed()
        for half in range(2):
            for i in range(3):
                if self.rows is None:
                    self.first(half, i).wait_send()
            for i in range(2):
                self.second(half, i, 0).wait_send()
                self.second(half, i, 1).wait_send()
                self.relay(half, i).wait_send()
            for i in range(5):
                self.across(half, i).wait_send()


class FirstRows(Gather):
    def __init__(self, own_ref, rows, send, recv, own_sem):
        seq = lax.axis_index("seq")
        self.chan = lax.axis_index("chan")
        self.own_ref, self.rows, self.send, self.recv, self.own_sem = (
            own_ref, rows, send, recv, own_sem
        )
        self.core = lax.rem(seq, 2)
        self.x = lax.rem(seq // 2, SIDE)
        self.y = seq // (2 * SIDE)
        self.half = own_ref.shape[0] // 2

    def first(self, half, i, landing=False):
        by = (1, -1, 2)[i]
        place = self.x if half == 0 else self.y
        if landing:
            place = lax.rem(place - by + SIDE, SIDE)
        src = self.own_ref.at[pl.ds(half * self.half, self.half)]
        index = half * 3 + i
        return remote(
            src, self.rows.at[half, place], self.send.at[index], self.recv.at[index],
            self.step(half, 1, by),
        )

    def local(self, half):
        src = self.own_ref.at[pl.ds(half * self.half, self.half)]
        place = self.x if half == 0 else self.y
        return pltpu.make_async_copy(src, self.rows.at[half, place], self.own_sem.at[half])

    def start(self):
        for half in range(2):
            for i in range(3):
                self.first(half, i).start()
            self.local(half).start()

    def end(self):
        for half in range(2):
            for i in range(3):
                self.first(half, i, True).wait()
            self.local(half).wait()


def gather_scratch():
    return [
        pltpu.SemaphoreType.DMA((COPIES,)),
        pltpu.SemaphoreType.DMA((COPIES,)),
        pltpu.SemaphoreType.DMA((2,)),
    ]


TILE = 128
GROUP = 16


def spread_taps(h_ref, base, ch):
    wide = jnp.broadcast_to(h_ref[ch], (8, h_ref.shape[2])).astype(F32)
    sub = lax.broadcasted_iota(jnp.int32, wide.shape, 0)
    for bit in (1, 2, 4):
        wide = jnp.where((sub & bit) != 0, pltpu.roll(wide, bit, 1), wide)
    base[...] = wide


def spread_signal(x_ref, shifted, ch):
    x = x_ref[ch].astype(F32)
    row = lax.broadcasted_iota(jnp.int32, x.shape, 0)
    for k in range(GROUP):
        moved = x if k == 0 else jnp.where(row >= k, pltpu.roll(x, k, 0), 0.0)
        lanes = pl.ds((k % AT_ONCE) * TILE, TILE)
        shifted[k // AT_ONCE, :, lanes] = moved.astype(BF16)


AT_ONCE = 4


def toeplitz(base, lane):
    window = base[:, pl.ds(pl.multiple_of(lane, TILE), (AT_ONCE + 1) * TILE)]
    moved = [window if u == 0 else pltpu.roll(window, 8 * u, 1) for u in range(TILE // 8)]
    parts = []
    for d in range(AT_ONCE):
        parts += [m[:, (d + 1) * TILE : (d + 2) * TILE] for m in moved]
    return jnp.concatenate(parts, axis=0).astype(BF16)


def convolve_group(base, shifted, total, g, blocks):
    rows = blocks - GROUP * g

    def some(kk, acc):
        block = toeplitz(base, (GROUP * g + AT_ONCE * kk) * TILE)
        left = shifted[kk, pl.ds(0, rows), :]
        return acc + jnp.dot(left, block, preferred_element_type=F32)

    acc = lax.fori_loop(0, GROUP // AT_ONCE, some, jnp.zeros((rows, TILE), F32), unroll=2)
    if g == 0:
        total[...] = acc
    else:
        total[pl.ds(GROUP * g, rows), :] += acc


def conv_and_keys(x, h, rows):
    tokens, head = 2 * rows.shape[2], rows.shape[3]

    def kernel(
        x_ref, h_ref, k_ref, y_ref, keys_out, buf, base, shifted, total, send, recv, own, away
    ):
        gather = Gather(None, buf, send, recv, own, k_ref)

        def write_out(index, core):
            return pltpu.make_async_copy(
                buf.at[:, :, core], keys_out.at[:, :, core], away.at[index]
            )

        pl.semaphore_wait(pltpu.get_barrier_semaphore(), gather.greet())
        gather.start()
        stages = {(0, 3): gather.late, (1, 0): gather.last}
        for ch in range(x_ref.shape[0]):
            spread_taps(h_ref, base, ch)
            spread_signal(x_ref, shifted, ch)
            for g in range(x_ref.shape[1] // GROUP):
                convolve_group(base, shifted, total, g, x_ref.shape[1])
                if (ch, g) in stages:
                    stages[ch, g]()
                if (ch, g) == (1, 0):
                    gather.placed()
                    write_out(0, gather.core).start()
            y_ref[ch] = total[...].astype(BF16)
        for half in range(2):
            gather.arrived(half)
        write_out(1, 1 - gather.core).start()
        gather.end()
        write_out(0, gather.core).wait()
        write_out(1, 1 - gather.core).wait()

    blocks = x.shape[1]
    return pl.pallas_call(
        kernel,
        out_shape=(
            jax.ShapeDtypeStruct(x.shape, BF16),
            jax.ShapeDtypeStruct((SIDE, SIDE, 2, tokens, head), BF16),
        ),
        in_specs=[pl.BlockSpec(memory_space=VM)] * 3,
        out_specs=(pl.BlockSpec(memory_space=VM), pl.BlockSpec(memory_space=pl.ANY)),
        scratch_shapes=[
            pltpu.VMEM((SIDE, SIDE, 2, tokens, head), BF16),
            pltpu.VMEM((8, h.shape[2]), F32),
            pltpu.VMEM((GROUP // AT_ONCE, blocks, AT_ONCE * TILE), BF16),
            pltpu.VMEM((blocks, TILE), F32),
        ]
        + gather_scratch()
        + [pltpu.SemaphoreType.DMA((2,))],
        compiler_params=pltpu.CompilerParams(collective_id=1, has_side_effects=True),
    )(x, h, rows)


QROWS = 128
SLICE = 32
UNROLL = 2


def key_block(buf, index, slab):
    part = buf[:, :, :, pl.ds(pl.multiple_of(index * slab, slab), slab), :]
    return part.reshape(2 * SIDE * SIDE * slab, part.shape[-1])


class Ring:
    def __init__(self, n, src, held, send, recv, own):
        self.n, self.src, self.held, self.send, self.recv, self.own = n, src, held, send, recv, own
        self.seq = lax.axis_index("seq")
        self.me = lax.axis_index("chan")
        self.steps = n // 2

    def greet(self):
        signal(device_at(self.seq, lax.rem(self.me + 1, self.n)))
        signal(device_at(self.seq, lax.rem(self.me + self.n - 1, self.n)))
        return 2

    def copy(self, k, side, landing=False):
        way = (1, -1)[side]
        away = k if landing else k - 1
        block = lax.rem(self.me - way * away + self.n, self.n)
        half = self.src.shape[0] // 2
        rows = pl.ds(side * half, half) if k == self.steps else pl.ds(0, 2 * half)
        dst = self.held.at[block, rows]
        src = self.src.at[rows] if k == 1 else dst
        index = 2 * (k - 1) + side
        target = device_at(self.seq, lax.rem(self.me + way + self.n, self.n))
        return remote(src, dst, self.send.at[index], self.recv.at[index], target)

    def start(self, k):
        if k == 1:
            self.local = pltpu.make_async_copy(self.src, self.held.at[self.me], self.own)
            self.local.start()
        for side in range(2):
            if k > 1:
                self.copy(k - 1, side, True).wait_recv()
            self.copy(k, side).start()

    def end(self):
        for side in range(2):
            self.copy(self.steps, side, True).wait_recv()
        self.local.wait()
        for k in range(1, self.steps + 1):
            for side in range(2):
                self.copy(k, side).wait_send()


def attend(queries, keys, mixed, w_value, slab, n_chan):
    tokens, head = queries.shape
    scale = math.log2(math.e) / math.sqrt(head)
    width = 2 * SIDE * SIDE * slab
    per_tile = QROWS // slab
    groups = width // TILE
    pv_blocks = 2

    def kernel(
        q_ref, k_far, m_ref, w_ref, out, k_buf, buf, weights, best, totals, acc, held, value,
        send, recv, own, ring_send, ring_recv, ring_own, fetched,
    ):
        first_row = lax.axis_index("seq") * slab
        row = lax.broadcasted_iota(jnp.int32, (QROWS, TILE), 0)
        lane = lax.broadcasted_iota(jnp.int32, (QROWS, TILE), 1)
        limit = (row // slab) * width + first_row + row % slab - lane

        def scores(tile, block):
            q = q_ref[pl.ds(tile * QROWS, tokens - tile * QROWS), :]
            return lax.dot_general(
                q, key_block(k_buf, block, slab), (((1,), (1,)), ((), ())),
                preferred_element_type=F32,
            )

        def allowed(tile, block, part):
            return (block - tile * per_tile) * width + part * TILE <= limit

        def edge(tile, block, part, start, values, other):
            if start >= QROWS:
                return values
            here = allowed(tile, block, part)[start : start + SLICE]
            return jnp.where(here, values, other)

        def find_best(tile, low, high):
            def one(block, carry):
                s = scores(tile, block)
                for start in range(0, s.shape[0], SLICE):
                    rows = pl.ds(tile * QROWS + start, SLICE)
                    top = best[rows, :]
                    for part in range(groups):
                        piece = s[start : start + SLICE, part * TILE : (part + 1) * TILE]
                        top = jnp.maximum(top, edge(tile, block, part, start, piece, -1e30))
                    best[rows, :] = top
                return carry

            lax.fori_loop(tile * per_tile + low, tile * per_tile + high, one, 0, unroll=UNROLL)

        def weigh(tile, low, high):
            def one(block, carry):
                s = scores(tile, block)
                for start in range(0, s.shape[0], SLICE):
                    rows = pl.ds(tile * QROWS + start, SLICE)
                    top = best[rows, :]
                    total = totals[rows, :]
                    for part in range(groups):
                        piece = s[start : start + SLICE, part * TILE : (part + 1) * TILE]
                        w = jnp.exp2((piece - top) * scale)
                        w = edge(tile, block, part, start, w, 0.0)
                        lanes = pl.ds(pl.multiple_of(block * width + part * TILE, TILE), TILE)
                        weights[rows, lanes] = w.astype(BF16)
                        total = total + w
                    totals[rows, :] = total
                return carry

            lax.fori_loop(tile * per_tile + low, tile * per_tile + high, one, 0, unroll=UNROLL)

        fetch = pltpu.make_async_copy(k_far, k_buf, fetched)
        fetch.start()
        ring = Ring(n_chan, m_ref, held, ring_send, ring_recv, ring_own)
        gather = Gather(value, buf, send, recv, own)
        greeted = ring.greet() + gather.greet()
        pl.semaphore_wait(pltpu.get_barrier_semaphore(), greeted)

        ring.start(1)
        best[...] = jnp.full(best.shape, -1e30, F32)
        totals[...] = jnp.zeros(totals.shape, F32)
        fetch.wait()
        find_best(0, 0, 4)
        ring.start(2)
        find_best(0, 4, 8)
        ring.start(3)
        find_best(1, 0, 8)
        ring.start(4)
        find_best(2, 0, 8)
        find_best(3, 0, 8)
        best[...] = jnp.broadcast_to(jnp.max(best[...], axis=1, keepdims=True), best.shape)
        ring.end()
        value[...] = lax.dot_general(
            held[...].reshape(held.shape[0] * held.shape[1], tokens),
            w_ref[...],
            (((0,), (0,)), ((), ())),
            preferred_element_type=F32,
        ).astype(BF16)
        weigh(3, 0, 2)
        gather.start()
        weigh(3, 2, 8)
        weigh(2, 0, 8)
        weigh(1, 0, 4)
        gather.middle()
        weigh(1, 4, 8)
        weigh(0, 0, 4)
        gather.late()
        weigh(0, 4, 8)
        acc[...] = jnp.zeros(acc.shape, F32)
        gather.last()
        for tile in range(tokens // QROWS):
            if tile == 0:
                gather.arrived(0)
            if 2 * tile * QROWS == tokens:
                gather.arrived(1)
            rows = pl.ds(tile * QROWS, tokens - tile * QROWS)

            def add(step, carry, rows=rows, tile=tile):
                block = tile * per_tile + step * pv_blocks
                lanes = pl.ds(pl.multiple_of(block * width, width), pv_blocks * width)
                right = jnp.concatenate(
                    [key_block(buf, block + i, slab) for i in range(pv_blocks)], axis=0
                )
                acc[rows, :] += jnp.dot(weights[rows, lanes], right, preferred_element_type=F32)
                return carry

            lax.fori_loop(0, per_tile // pv_blocks, add, 0, unroll=UNROLL)
        gather.end()
        total = jnp.sum(totals[...], axis=1, keepdims=True)
        out[...] = (acc[...] / total).astype(BF16)

    return pl.pallas_call(
        kernel,
        out_shape=jax.ShapeDtypeStruct((tokens, head), BF16),
        in_specs=[pl.BlockSpec(memory_space=pl.ANY if i == 1 else VM) for i in range(4)],
        out_specs=pl.BlockSpec(memory_space=VM),
        scratch_shapes=[
            pltpu.VMEM((SIDE, SIDE, 2, tokens, head), BF16),
            pltpu.VMEM((SIDE, SIDE, 2, tokens, head), BF16),
            pltpu.VMEM((tokens, tokens * 2 * SIDE * SIDE), BF16),
            pltpu.VMEM((tokens, TILE), F32),
            pltpu.VMEM((tokens, TILE), F32),
            pltpu.VMEM((tokens, head), F32),
            pltpu.VMEM((n_chan,) + mixed.shape, BF16),
            pltpu.VMEM((tokens, head), BF16),
        ]
        + gather_scratch()
        + [
            pltpu.SemaphoreType.DMA((n_chan,)),
            pltpu.SemaphoreType.DMA((n_chan,)),
            pltpu.SemaphoreType.DMA,
            pltpu.SemaphoreType.DMA,
        ],
        compiler_params=pltpu.CompilerParams(collective_id=2, has_side_effects=True),
    )(queries, keys, mixed, w_value)


def body(n_chan, conv_in, conv_gate, long_filter, skip_gain, queries, keys_in, w_value):
    blocks, slab, channels = conv_in.shape
    tokens = blocks * slab
    n_seq = 2 * SIDE * SIDE
    each = channels // n_seq
    length = tokens * n_seq
    lines = tokens // TILE
    signal_t = conv_in.reshape(tokens, channels).T
    taps_t = long_filter.reshape(tokens, channels).astype(BF16).T
    packed = jnp.stack(
        [signal_t.reshape(n_seq, each, tokens), taps_t.reshape(n_seq, each, tokens)], axis=1
    ).reshape(n_seq, 2 * each * lines, TILE)
    got, rows = exchange_and_rows(packed, keys_in.reshape(tokens, -1))
    whole = (
        got.reshape(n_seq, 2, each, blocks, slab).transpose(1, 2, 3, 0, 4).reshape(2, each, length)
    )
    x = whole[0].reshape(each, length // TILE, TILE)
    h = jnp.pad(whole[1].astype(F32), ((0, 0), (TILE, 0))).reshape(each, 1, length + TILE)
    y, keys = conv_and_keys(x, h, rows)
    back = (
        y.reshape(each, blocks, n_seq, slab)
        .transpose(2, 0, 1, 3)
        .reshape(n_seq, each * lines, TILE)
    )
    convolved = all_to_all(back, 4).reshape(channels, tokens).astype(F32)
    gate_t = conv_gate.reshape(tokens, channels).T
    mixed_t = (
        (convolved + skip_gain[:, None] * signal_t.astype(F32)) * gate_t.astype(F32)
    ).astype(BF16)
    conv_out = mixed_t.T.reshape(blocks, slab, channels)
    attended = attend(queries.reshape(tokens, -1), keys, mixed_t, w_value, slab, n_chan)
    return conv_out, attended.reshape(blocks, slab, -1)


def solution(mesh):
    n_chan = mesh.shape["chan"]

    def local(*args):
        return body(n_chan, *args)

    spec = P(None, "seq", "chan")
    return jax.shard_map(
        local,
        mesh=mesh,
        in_specs=(spec, spec, spec, P("chan"), spec, spec, P(None, "chan")),
        out_specs=(spec, spec),
        check_vma=False,
    )
```

```python
import math

import jax
import jax.numpy as jnp
from jax import lax
from jax.experimental import pallas as pl
from jax.experimental.pallas import tpu as pltpu
from jax.sharding import PartitionSpec as P

MESH = pl.DeviceIdType.MESH
F32 = jnp.float32
BF16 = jnp.bfloat16
VM = pltpu.VMEM


def device_at(seq, chan):
    return (jnp.int32(seq), jnp.int32(chan))


def signal(target):
    pl.semaphore_signal(
        pltpu.get_barrier_semaphore(), inc=1, device_id=target, device_id_type=MESH
    )


def remote(src, dst, send, recv, target):
    return pltpu.make_async_remote_copy(
        src_ref=src,
        dst_ref=dst,
        send_sem=send,
        recv_sem=recv,
        device_id=target,
        device_id_type=MESH,
    )


def exchange_kernel(n, src, dst, send, recv, own, beside=None):
    seq = lax.axis_index("seq")
    chan = lax.axis_index("chan")
    me = seq

    def peer(step):
        other = lax.rem(me + step, n)
        return other, device_at(other, chan)

    def greet(step, carry):
        signal(peer(step)[1])
        return carry

    lax.fori_loop(1, n, greet, 0)
    local = pltpu.make_async_copy(src.at[me], dst.at[me], own)
    local.start()
    pl.semaphore_wait(pltpu.get_barrier_semaphore(), n - 1)

    def post(step, carry):
        other, target = peer(step)
        remote(src.at[other], dst.at[me], send.at[step], recv.at[step], target).start()
        return carry

    lax.fori_loop(1, n, post, 0)
    if beside is not None:
        beside.start()

    def finish(step, carry):
        other, target = peer(step)
        back = lax.rem(me + n - step, n)
        remote(src.at[other], dst.at[back], send.at[step], recv.at[step], target).wait()
        return carry

    lax.fori_loop(1, n, finish, 0)
    local.wait()
    if beside is not None:
        beside.end()


def exchange_scratch(n):
    return [
        pltpu.SemaphoreType.DMA((n,)),
        pltpu.SemaphoreType.DMA((n,)),
        pltpu.SemaphoreType.DMA,
    ]


def all_to_all(blocks, collective):
    n = blocks.shape[0]

    def kernel(src, dst, send, recv, own):
        exchange_kernel(n, src, dst, send, recv, own)

    return pl.pallas_call(
        kernel,
        out_shape=jax.ShapeDtypeStruct(blocks.shape, blocks.dtype),
        in_specs=[pl.BlockSpec(memory_space=VM)],
        out_specs=pl.BlockSpec(memory_space=VM),
        scratch_shapes=exchange_scratch(n),
        compiler_params=pltpu.CompilerParams(collective_id=collective, has_side_effects=True),
    )(blocks)


def exchange_and_rows(blocks, keys):
    n = blocks.shape[0]
    tokens, head = keys.shape

    def kernel(src, k_ref, dst, rows, send, recv, own, row_send, row_recv, row_own):
        beside = FirstRows(k_ref, rows, row_send, row_recv, row_own)
        exchange_kernel(n, src, dst, send, recv, own, beside)

    return pl.pallas_call(
        kernel,
        out_shape=(
            jax.ShapeDtypeStruct(blocks.shape, blocks.dtype),
            jax.ShapeDtypeStruct((2, SIDE, tokens // 2, head), BF16),
        ),
        in_specs=[pl.BlockSpec(memory_space=VM)] * 2,
        out_specs=(pl.BlockSpec(memory_space=VM),) * 2,
        scratch_shapes=exchange_scratch(n)
        + [
            pltpu.SemaphoreType.DMA((6,)),
            pltpu.SemaphoreType.DMA((6,)),
            pltpu.SemaphoreType.DMA((2,)),
        ],
        compiler_params=pltpu.CompilerParams(collective_id=0, has_side_effects=True),
    )(blocks, keys)


SIDE = 4
COPIES = 28


class Gather:
    def __init__(self, own_ref, buf, send, recv, own_sem, rows=None):
        seq = lax.axis_index("seq")
        self.rows = rows
        self.chan = lax.axis_index("chan")
        self.own_ref, self.buf, self.send, self.recv, self.own_sem = (
            own_ref, buf, send, recv, own_sem
        )
        self.core = lax.rem(seq, 2)
        self.x = lax.rem(seq // 2, SIDE)
        self.y = seq // (2 * SIDE)
        self.half = buf.shape[3] // 2

    def at(self, y, x, core):
        return device_at((y * SIDE + x) * 2 + core, self.chan)

    def step(self, half, phase, by):
        along_x = (half == 0) == (phase == 1)
        if along_x:
            return self.at(self.y, lax.rem(self.x + by + SIDE, SIDE), self.core)
        return self.at(lax.rem(self.y + by + SIDE, SIDE), self.x, self.core)

    def block(self, half, phase, by):
        rows = pl.ds(half * self.half, self.half)
        along_x = (half == 0) == (phase == 1)
        y, x = self.y, self.x
        if along_x:
            x = lax.rem(x + by + SIDE, SIDE)
        else:
            y = lax.rem(y + by + SIDE, SIDE)
        return y, x, along_x, rows

    def one(self, half, by):
        y, x, _, rows = self.block(half, 1, by)
        return self.buf.at[y, x, self.core, rows]

    def row(self, half, by, core=None, part=None):
        y, x, along_x, rows = self.block(half, 2, by)
        core = self.core if core is None else core
        if part is not None:
            quarter = self.half // 2
            rows = pl.ds(half * self.half + part * quarter, quarter)
        if along_x:
            return self.buf.at[:, x, core, rows]
        return self.buf.at[y, :, core, rows]

    def sems(self, half, number):
        index = half * 14 + number
        return self.send.at[index], self.recv.at[index]

    def held(self, half, part=None):
        if self.rows is None:
            return self.row(half, 0, part=part)
        if part is None:
            return self.rows.at[half]
        return self.rows.at[half, :, pl.ds(part * (self.half // 2), self.half // 2)]

    def greet(self):
        places = (1, 2, 3) if self.rows is None else (1, 3)
        for by in places:
            signal(self.step(0, 1, by))
            signal(self.step(1, 1, by))
        signal(self.at(self.y, self.x, 1 - self.core))
        return 2 * len(places) + 1


    def first(self, half, i, landing=False):
        by = (1, -1, 2)[i]
        rows = pl.ds(half * self.half, self.half)
        dst = self.one(half, -by) if landing else self.one(half, 0)
        return remote(self.own_ref.at[rows], dst, *self.sems(half, i), self.step(half, 1, by))

    def second(self, half, i, part, landing=False):
        by = (1, -1)[i]
        dst = self.row(half, -by if landing else 0, part=part)
        return remote(self.held(half, part), dst, *self.sems(half, 3 + 2 * i + part), self.step(half, 2, by))

    def relay(self, half, i, landing=False):
        by = (1, -1)[i]
        src = self.row(half, -by, part=i)
        dst = self.row(half, 2, part=i) if landing else src
        return remote(src, dst, *self.sems(half, 7 + i), self.step(half, 2, by))

    def across(self, half, i, landing=False):
        by, part = ((0, None), (-1, None), (1, None), (2, 0), (2, 1))[i]
        src = self.held(half) if i == 0 else self.row(half, by, part=part)
        dst = self.row(half, by, core=1 - self.core if landing else self.core, part=part)
        return remote(
            src, dst, *self.sems(half, 9 + i), self.at(self.y, self.x, 1 - self.core)
        )

    def start(self):
        if self.rows is not None:
            self.local = [
                pltpu.make_async_copy(self.held(half), self.row(half, 0), self.own_sem.at[half])
                for half in range(2)
            ]
            for copy in self.local:
                copy.start()
            self.post()
            return
        copy = pltpu.make_async_copy(
            self.own_ref, self.buf.at[self.y, self.x, self.core], self.own_sem.at[0]
        )
        copy.start()
        self.local = [copy]
        for i in range(3):
            for half in range(2):
                self.first(half, i).start()

    def middle(self):
        self.local.pop().wait()
        for half in range(2):
            for i in range(3):
                self.first(half, i, True).wait_recv()
        self.post()

    def post(self):
        for half in range(2):
            for i in range(2):
                self.second(half, i, i).start()
        for half in range(2):
            for i in range(2):
                self.second(half, i, 1 - i).start()
            self.across(half, 0).start()

    def late(self):
        for half in range(2):
            for i in range(2):
                self.second(half, i, i, True).wait_recv()
                self.relay(half, i).start()

    def last(self):
        for half in range(2):
            for i in range(2):
                self.second(half, i, 1 - i, True).wait_recv()
                self.across(half, 1 + i).start()
        for half in range(2):
            for i in range(2):
                self.relay(half, i, True).wait_recv()
                self.across(half, 3 + i).start()

    def arrived(self, half):
        for i in range(5):
            self.across(half, i, True).wait_recv()

    def placed(self):
        while self.local:
            self.local.pop().wait()

    def end(self):
        self.placed()
        for half in range(2):
            for i in range(3):
                if self.rows is None:
                    self.first(half, i).wait_send()
            for i in range(2):
                self.second(half, i, 0).wait_send()
                self.second(half, i, 1).wait_send()
                self.relay(half, i).wait_send()
            for i in range(5):
                self.across(half, i).wait_send()


class FirstRows(Gather):
    def __init__(self, own_ref, rows, send, recv, own_sem):
        seq = lax.axis_index("seq")
        self.chan = lax.axis_index("chan")
        self.own_ref, self.rows, self.send, self.recv, self.own_sem = (
            own_ref, rows, send, recv, own_sem
        )
        self.core = lax.rem(seq, 2)
        self.x = lax.rem(seq // 2, SIDE)
        self.y = seq // (2 * SIDE)
        self.half = own_ref.shape[0] // 2

    def first(self, half, i, landing=False):
        by = (1, -1, 2)[i]
        place = self.x if half == 0 else self.y
        if landing:
            place = lax.rem(place - by + SIDE, SIDE)
        src = self.own_ref.at[pl.ds(half * self.half, self.half)]
        index = half * 3 + i
        return remote(
            src, self.rows.at[half, place], self.send.at[index], self.recv.at[index],
            self.step(half, 1, by),
        )

    def local(self, half):
        src = self.own_ref.at[pl.ds(half * self.half, self.half)]
        place = self.x if half == 0 else self.y
        return pltpu.make_async_copy(src, self.rows.at[half, place], self.own_sem.at[half])

    def start(self):
        for half in range(2):
            for i in range(3):
                self.first(half, i).start()
            self.local(half).start()

    def end(self):
        for half in range(2):
            for i in range(3):
                self.first(half, i, True).wait()
            self.local(half).wait()


def gather_scratch():
    return [
        pltpu.SemaphoreType.DMA((COPIES,)),
        pltpu.SemaphoreType.DMA((COPIES,)),
        pltpu.SemaphoreType.DMA((2,)),
    ]


TILE = 128
GROUP = 16


def spread_taps(h_ref, base, ch):
    wide = jnp.broadcast_to(h_ref[ch], (8, h_ref.shape[2])).astype(F32)
    sub = lax.broadcasted_iota(jnp.int32, wide.shape, 0)
    for bit in (1, 2, 4):
        wide = jnp.where((sub & bit) != 0, pltpu.roll(wide, bit, 1), wide)
    base[...] = wide


def spread_signal(x_ref, shifted, ch):
    x = x_ref[ch].astype(F32)
    row = lax.broadcasted_iota(jnp.int32, x.shape, 0)
    for k in range(GROUP):
        moved = x if k == 0 else jnp.where(row >= k, pltpu.roll(x, k, 0), 0.0)
        lanes = pl.ds((k % AT_ONCE) * TILE, TILE)
        shifted[k // AT_ONCE, :, lanes] = moved.astype(BF16)


AT_ONCE = 4


def toeplitz(base, lane):
    window = base[:, pl.ds(pl.multiple_of(lane, TILE), (AT_ONCE + 1) * TILE)]
    moved = [window if u == 0 else pltpu.roll(window, 8 * u, 1) for u in range(TILE // 8)]
    parts = []
    for d in range(AT_ONCE):
        parts += [m[:, (d + 1) * TILE : (d + 2) * TILE] for m in moved]
    return jnp.concatenate(parts, axis=0).astype(BF16)


def convolve_group(base, shifted, total, g, blocks):
    rows = blocks - GROUP * g

    def some(kk, acc):
        block = toeplitz(base, (GROUP * g + AT_ONCE * kk) * TILE)
        left = shifted[kk, pl.ds(0, rows), :]
        return acc + jnp.dot(left, block, preferred_element_type=F32)

    acc = lax.fori_loop(0, GROUP // AT_ONCE, some, jnp.zeros((rows, TILE), F32), unroll=2)
    if g == 0:
        total[...] = acc
    else:
        total[pl.ds(GROUP * g, rows), :] += acc


def conv_and_keys(x, h, rows):
    tokens, head = 2 * rows.shape[2], rows.shape[3]

    def kernel(
        x_ref, h_ref, k_ref, y_ref, keys_out, buf, base, shifted, total, send, recv, own, away
    ):
        gather = Gather(None, buf, send, recv, own, k_ref)

        def write_out(index, core):
            return pltpu.make_async_copy(
                buf.at[:, :, core], keys_out.at[:, :, core], away.at[index]
            )

        pl.semaphore_wait(pltpu.get_barrier_semaphore(), gather.greet())
        gather.start()
        stages = {(0, 3): gather.late, (1, 2): gather.last}
        for ch in range(x_ref.shape[0]):
            spread_taps(h_ref, base, ch)
            spread_signal(x_ref, shifted, ch)
            for g in range(x_ref.shape[1] // GROUP):
                convolve_group(base, shifted, total, g, x_ref.shape[1])
                if (ch, g) in stages:
                    stages[ch, g]()
                if (ch, g) == (1, 2):
                    gather.placed()
                    write_out(0, gather.core).start()
            y_ref[ch] = total[...].astype(BF16)
        for half in range(2):
            gather.arrived(half)
        write_out(1, 1 - gather.core).start()
        gather.end()
        write_out(0, gather.core).wait()
        write_out(1, 1 - gather.core).wait()

    blocks = x.shape[1]
    return pl.pallas_call(
        kernel,
        out_shape=(
            jax.ShapeDtypeStruct(x.shape, BF16),
            jax.ShapeDtypeStruct((SIDE, SIDE, 2, tokens, head), BF16),
        ),
        in_specs=[pl.BlockSpec(memory_space=VM)] * 3,
        out_specs=(pl.BlockSpec(memory_space=VM), pl.BlockSpec(memory_space=pl.ANY)),
        scratch_shapes=[
            pltpu.VMEM((SIDE, SIDE, 2, tokens, head), BF16),
            pltpu.VMEM((8, h.shape[2]), F32),
            pltpu.VMEM((GROUP // AT_ONCE, blocks, AT_ONCE * TILE), BF16),
            pltpu.VMEM((blocks, TILE), F32),
        ]
        + gather_scratch()
        + [pltpu.SemaphoreType.DMA((2,))],
        compiler_params=pltpu.CompilerParams(collective_id=1, has_side_effects=True),
    )(x, h, rows)


QROWS = 128
SLICE = 32
UNROLL = 2


def key_block(buf, index, slab):
    part = buf[:, :, :, pl.ds(pl.multiple_of(index * slab, slab), slab), :]
    return part.reshape(2 * SIDE * SIDE * slab, part.shape[-1])


class Ring:
    def __init__(self, n, src, held, send, recv, own):
        self.n, self.src, self.held, self.send, self.recv, self.own = n, src, held, send, recv, own
        self.seq = lax.axis_index("seq")
        self.me = lax.axis_index("chan")
        self.steps = n // 2

    def greet(self):
        signal(device_at(self.seq, lax.rem(self.me + 1, self.n)))
        signal(device_at(self.seq, lax.rem(self.me + self.n - 1, self.n)))
        return 2

    def copy(self, k, side, landing=False):
        way = (1, -1)[side]
        away = k if landing else k - 1
        block = lax.rem(self.me - way * away + self.n, self.n)
        half = self.src.shape[0] // 2
        rows = pl.ds(side * half, half) if k == self.steps else pl.ds(0, 2 * half)
        dst = self.held.at[block, rows]
        src = self.src.at[rows] if k == 1 else dst
        index = 2 * (k - 1) + side
        target = device_at(self.seq, lax.rem(self.me + way + self.n, self.n))
        return remote(src, dst, self.send.at[index], self.recv.at[index], target)

    def start(self, k):
        if k == 1:
            self.local = pltpu.make_async_copy(self.src, self.held.at[self.me], self.own)
            self.local.start()
        for side in range(2):
            if k > 1:
                self.copy(k - 1, side, True).wait_recv()
            self.copy(k, side).start()

    def end(self):
        for side in range(2):
            self.copy(self.steps, side, True).wait_recv()
        self.local.wait()
        for k in range(1, self.steps + 1):
            for side in range(2):
                self.copy(k, side).wait_send()


def attend(queries, keys, mixed, w_value, slab, n_chan):
    tokens, head = queries.shape
    scale = math.log2(math.e) / math.sqrt(head)
    width = 2 * SIDE * SIDE * slab
    per_tile = QROWS // slab
    groups = width // TILE
    pv_blocks = 2

    def kernel(
        q_ref, k_far, m_ref, w_ref, out, k_buf, buf, weights, best, totals, acc, held, value,
        send, recv, own, ring_send, ring_recv, ring_own, fetched,
    ):
        first_row = lax.axis_index("seq") * slab
        row = lax.broadcasted_iota(jnp.int32, (QROWS, TILE), 0)
        lane = lax.broadcasted_iota(jnp.int32, (QROWS, TILE), 1)
        limit = (row // slab) * width + first_row + row % slab - lane

        def scores(tile, block):
            q = q_ref[pl.ds(tile * QROWS, tokens - tile * QROWS), :]
            return lax.dot_general(
                q, key_block(k_buf, block, slab), (((1,), (1,)), ((), ())),
                preferred_element_type=F32,
            )

        def allowed(tile, block, part):
            return (block - tile * per_tile) * width + part * TILE <= limit

        def edge(tile, block, part, start, values, other):
            if start >= QROWS:
                return values
            here = allowed(tile, block, part)[start : start + SLICE]
            return jnp.where(here, values, other)

        def find_best(tile, low, high):
            def one(block, carry):
                s = scores(tile, block)
                for start in range(0, s.shape[0], SLICE):
                    rows = pl.ds(tile * QROWS + start, SLICE)
                    top = best[rows, :]
                    for part in range(groups):
                        piece = s[start : start + SLICE, part * TILE : (part + 1) * TILE]
                        top = jnp.maximum(top, edge(tile, block, part, start, piece, -1e30))
                    best[rows, :] = top
                return carry

            lax.fori_loop(tile * per_tile + low, tile * per_tile + high, one, 0, unroll=UNROLL)

        def weigh(tile, low, high):
            def one(block, carry):
                s = scores(tile, block)
                for start in range(0, s.shape[0], SLICE):
                    rows = pl.ds(tile * QROWS + start, SLICE)
                    top = best[rows, :]
                    total = totals[rows, :]
                    for part in range(groups):
                        piece = s[start : start + SLICE, part * TILE : (part + 1) * TILE]
                        w = jnp.exp2((piece - top) * scale)
                        w = edge(tile, block, part, start, w, 0.0)
                        lanes = pl.ds(pl.multiple_of(block * width + part * TILE, TILE), TILE)
                        weights[rows, lanes] = w.astype(BF16)
                        total = total + w
                    totals[rows, :] = total
                return carry

            lax.fori_loop(tile * per_tile + low, tile * per_tile + high, one, 0, unroll=UNROLL)

        fetch = pltpu.make_async_copy(k_far, k_buf, fetched)
        fetch.start()
        ring = Ring(n_chan, m_ref, held, ring_send, ring_recv, ring_own)
        gather = Gather(value, buf, send, recv, own)
        greeted = ring.greet() + gather.greet()
        pl.semaphore_wait(pltpu.get_barrier_semaphore(), greeted)

        ring.start(1)
        best[...] = jnp.full(best.shape, -1e30, F32)
        totals[...] = jnp.zeros(totals.shape, F32)
        fetch.wait()
        find_best(0, 0, 4)
        ring.start(2)
        find_best(0, 4, 8)
        ring.start(3)
        find_best(1, 0, 8)
        ring.start(4)
        find_best(2, 0, 8)
        find_best(3, 0, 8)
        best[...] = jnp.broadcast_to(jnp.max(best[...], axis=1, keepdims=True), best.shape)
        ring.end()
        value[...] = lax.dot_general(
            held[...].reshape(held.shape[0] * held.shape[1], tokens),
            w_ref[...],
            (((0,), (0,)), ((), ())),
            preferred_element_type=F32,
        ).astype(BF16)
        weigh(3, 0, 2)
        gather.start()
        weigh(3, 2, 8)
        weigh(2, 0, 8)
        gather.middle()
        weigh(1, 0, 8)
        gather.late()
        weigh(0, 0, 8)
        acc[...] = jnp.zeros(acc.shape, F32)
        gather.last()
        for tile in range(tokens // QROWS):
            if tile == 0:
                gather.arrived(0)
            if 2 * tile * QROWS == tokens:
                gather.arrived(1)
            rows = pl.ds(tile * QROWS, tokens - tile * QROWS)

            def add(step, carry, rows=rows, tile=tile):
                block = tile * per_tile + step * pv_blocks
                lanes = pl.ds(pl.multiple_of(block * width, width), pv_blocks * width)
                right = jnp.concatenate(
                    [key_block(buf, block + i, slab) for i in range(pv_blocks)], axis=0
                )
                acc[rows, :] += jnp.dot(weights[rows, lanes], right, preferred_element_type=F32)
                return carry

            lax.fori_loop(0, per_tile // pv_blocks, add, 0, unroll=UNROLL)
        gather.end()
        total = jnp.sum(totals[...], axis=1, keepdims=True)
        out[...] = (acc[...] / total).astype(BF16)

    return pl.pallas_call(
        kernel,
        out_shape=jax.ShapeDtypeStruct((tokens, head), BF16),
        in_specs=[pl.BlockSpec(memory_space=pl.ANY if i == 1 else VM) for i in range(4)],
        out_specs=pl.BlockSpec(memory_space=VM),
        scratch_shapes=[
            pltpu.VMEM((SIDE, SIDE, 2, tokens, head), BF16),
            pltpu.VMEM((SIDE, SIDE, 2, tokens, head), BF16),
            pltpu.VMEM((tokens, tokens * 2 * SIDE * SIDE), BF16),
            pltpu.VMEM((tokens, TILE), F32),
            pltpu.VMEM((tokens, TILE), F32),
            pltpu.VMEM((tokens, head), F32),
            pltpu.VMEM((n_chan,) + mixed.shape, BF16),
            pltpu.VMEM((tokens, head), BF16),
        ]
        + gather_scratch()
        + [
            pltpu.SemaphoreType.DMA((n_chan,)),
            pltpu.SemaphoreType.DMA((n_chan,)),
            pltpu.SemaphoreType.DMA,
            pltpu.SemaphoreType.DMA,
        ],
        compiler_params=pltpu.CompilerParams(collective_id=2, has_side_effects=True),
    )(queries, keys, mixed, w_value)


def body(n_chan, conv_in, conv_gate, long_filter, skip_gain, queries, keys_in, w_value):
    blocks, slab, channels = conv_in.shape
    tokens = blocks * slab
    n_seq = 2 * SIDE * SIDE
    each = channels // n_seq
    length = tokens * n_seq
    lines = tokens // TILE
    signal_t = conv_in.reshape(tokens, channels).T
    taps_t = long_filter.reshape(tokens, channels).astype(BF16).T
    packed = jnp.stack(
        [signal_t.reshape(n_seq, each, tokens), taps_t.reshape(n_seq, each, tokens)], axis=1
    ).reshape(n_seq, 2 * each * lines, TILE)
    got, rows = exchange_and_rows(packed, keys_in.reshape(tokens, -1))
    whole = (
        got.reshape(n_seq, 2, each, blocks, slab).transpose(1, 2, 3, 0, 4).reshape(2, each, length)
    )
    x = whole[0].reshape(each, length // TILE, TILE)
    h = jnp.pad(whole[1].astype(F32), ((0, 0), (TILE, 0))).reshape(each, 1, length + TILE)
    y, keys = conv_and_keys(x, h, rows)
    back = (
        y.reshape(each, blocks, n_seq, slab)
        .transpose(2, 0, 1, 3)
        .reshape(n_seq, each * lines, TILE)
    )
    convolved = all_to_all(back, 4).reshape(channels, tokens).astype(F32)
    gate_t = conv_gate.reshape(tokens, channels).T
    mixed_t = (
        (convolved + skip_gain[:, None] * signal_t.astype(F32)) * gate_t.astype(F32)
    ).astype(BF16)
    conv_out = mixed_t.T.reshape(blocks, slab, channels)
    attended = attend(queries.reshape(tokens, -1), keys, mixed_t, w_value, slab, n_chan)
    return conv_out, attended.reshape(blocks, slab, -1)


def solution(mesh):
    n_chan = mesh.shape["chan"]

    def local(*args):
        return body(n_chan, *args)

    spec = P(None, "seq", "chan")
    return jax.shard_map(
        local,
        mesh=mesh,
        in_specs=(spec, spec, spec, P("chan"), spec, spec, P(None, "chan")),
        out_specs=(spec, spec),
        check_vma=False,
    )
```
